512 devices in a mesh: grp: 4 (over x), slab: 128 (over z, y, core).
Axes of the slice: x: 4, y: 4, z: 16, core: 2. Of those that a mesh axis runs over, the one named last changes fastest.
Arguments:
- margin: bfloat16 [2048, 5, 128, 128], P(('grp', 'slab')), may hold values from -2 to 2
- factor: bfloat16 [2048, 5, 128, 128], P(('grp', 'slab')), may hold values from -2 to 2
- pattern: int32 [2048, 5], P(('grp', 'slab')), may hold values from 0 to 1, as said below
Outputs:
- refined: bfloat16 [2048, 5, 128, 128], P(('grp', 'slab'))
- defect_norm: float32 [], replicated
The draws below stay inside these ranges and needn't reach their ends.
Inputs may be any that keep to these rules, and one draw needn't show every extreme that they name: The pattern is symmetric: pattern[j, o] equals pattern[j + o - 2, 4 - o]. The diagonal block (o = 2) is always present and blocks whose row lies outside the matrix are absent; the share of present blocks varies from region to region.
All inputs are finite; a program needn't handle non-finite values.
Results may differ from the reference program's by a relative error of at most 0.0054.
Values may be sent and summed in bfloat16 or wider, within the bound.
A program may use at most 64 MiB of HBM per device.

```python
import jax
import jax.numpy as jnp
from jax import lax

B = 128
W = 2
CB = 4
QB = 512
NB = 2048


def rough_blocks(key, shape):
    return jax.random.truncated_normal(key, -4.0, 4.0, shape, jnp.float32)


def region_length():
    return max(QB // 2, 1)


def draw_margin(key, part):
    span = region_length()
    region_count = NB // span + 1
    log_level = jax.random.uniform(jax.random.fold_in(key, 103), (region_count,), jnp.float32, jnp.log(0.15), jnp.log(1.0))
    level = jnp.exp(log_level)
    growth = level[jnp.arange(NB) // span] / B ** 0.5
    upper_blocks = rough_blocks(jax.random.fold_in(key, 101), (NB, W, B, B)) * growth[:, None, None, None]
    diag_noise = rough_blocks(jax.random.fold_in(key, 102), (NB, B, B)) * (0.3 / B ** 0.5)
    diagonal = jnp.eye(B, dtype=jnp.float32)[None] + 0.5 * (diag_noise + jnp.swapaxes(diag_noise, 1, 2))
    pieces = []
    for distance in range(W, 0, -1):
        pieces.append(upper_blocks[:, distance - 1])
    pieces.append(diagonal)
    for distance in range(1, W + 1):
        shifted_up = jnp.concatenate([upper_blocks[distance:, distance - 1], jnp.zeros((distance, B, B), jnp.float32)], axis=0)
        pieces.append(jnp.swapaxes(shifted_up, 1, 2))
    return jnp.stack(pieces, axis=1).astype(jnp.bfloat16)


def draw_factor(key, part):
    spread_scale = 0.3
    blocks = rough_blocks(jax.random.fold_in(key, 201), (NB, 2 * W + 1, B, B)) * (spread_scale / B ** 0.5)
    centre = (jnp.arange(2 * W + 1) == W).astype(jnp.float32)[None, :, None, None] * jnp.eye(B, dtype=jnp.float32)[None, None]
    return (blocks + centre).astype(jnp.bfloat16)


def draw_pattern(key, part):
    span = region_length()
    region = jax.random.randint(jax.random.fold_in(key, 301), (NB // span + 1,), 3, 10)
    keep_level = region[jnp.arange(NB) // span]
    coin_draw = jax.random.randint(jax.random.fold_in(key, 302), (NB, W), 0, 10)
    upper_present = (coin_draw < keep_level[:, None]).astype(jnp.int32)
    column_index = jnp.arange(NB)
    pieces = []
    for distance in range(W, 0, -1):
        pieces.append(upper_present[:, distance - 1] * (column_index >= distance).astype(jnp.int32))
    pieces.append(jnp.ones((NB,), jnp.int32))
    for distance in range(1, W + 1):
        pieces.append(jnp.concatenate([upper_present[distance:, distance - 1], jnp.zeros((distance,), jnp.int32)], axis=0))
    return jnp.stack(pieces, axis=1).astype(jnp.int32)


def setup_inputs(seed: int = 0) -> dict:
    streams_of = jax.random.split(jax.random.key(seed), 4)
    return {
        "margin": draw_margin(jax.random.fold_in(streams_of[3], 71), 0),
        "factor": draw_factor(jax.random.fold_in(streams_of[3], 71), 0),
        "pattern": draw_pattern(jax.random.fold_in(streams_of[3], 71), 0),
    }


def image_terms(band_half):
    return [[(inner_lag, outer_lag - inner_lag + band_half, inner_lag + band_half) for inner_lag in range(max(-band_half, outer_lag - band_half), min(band_half, outer_lag + band_half) + 1)] for outer_lag in range(-2 * band_half, 2 * band_half + 1)]

def defect_terms(band_half):
    return [[(outer_lag, inner_lag - outer_lag + band_half, inner_lag + 2 * band_half) for inner_lag in range(outer_lag - band_half, outer_lag + band_half + 1)] for outer_lag in range(-band_half, band_half + 1)]

def near_terms(band_half):
    return [[(inner_lag, outer_lag - inner_lag + band_half, inner_lag + band_half) for inner_lag in range(max(-band_half, outer_lag - band_half), min(band_half, outer_lag + band_half) + 1)] for outer_lag in range(-band_half, band_half + 1)]

def band_product(left_ext, right_own, term_list, transpose_left, columns):
    left_stack = jnp.stack([left_ext[W + column_shift:W + column_shift + columns, left_offset] for column_shift, left_offset, right_offset in term_list], axis=1).astype(jnp.float32)
    right_stack = jnp.stack([right_own[:, right_offset] for column_shift, left_offset, right_offset in term_list], axis=1).astype(jnp.float32)
    einsum_form = 'cbkm,cbkn->cmn' if transpose_left else 'cbmk,cbkn->cmn'
    return jnp.einsum(einsum_form, left_stack, right_stack)

def stack_offsets(left_ext, right_own, term_lists, transpose_left, columns):
    outputs = [band_product(left_ext, right_own, term_list, transpose_left, columns) for term_list in term_lists]
    return jnp.stack(outputs, axis=1)

def reference(margin, factor, pattern):
    present = pattern.astype(jnp.bfloat16)[:, :, None, None]
    block_rows = jnp.arange(NB, dtype=jnp.int32)[:, None] + jnp.arange(2 * W + 1, dtype=jnp.int32)[None, :] - W
    own_quarter = (jnp.arange(NB, dtype=jnp.int32) // QB)[:, None]
    in_quarter = (block_rows // QB == own_quarter).astype(jnp.bfloat16)[:, :, None, None]
    s_eff = margin * present
    z_eff = factor * present * in_quarter
    centre = (jnp.arange(2 * W + 1, dtype=jnp.int32) == W).astype(jnp.float32)[None, :, None, None] * jnp.eye(B, dtype=jnp.float32)[None, None]
    pad_spec = ((W, W), (0, 0), (0, 0), (0, 0))
    s_pad = jnp.pad(s_eff, pad_spec)
    z_pad = jnp.pad(z_eff, pad_spec)
    group_ids = jnp.arange(NB // CB, dtype=jnp.int32)

    def first_pass(group):
        start = (group * CB).astype(jnp.int32)
        s_ext = lax.dynamic_slice_in_dim(s_pad, start, CB + 2 * W, 0)
        z_ext = lax.dynamic_slice_in_dim(z_pad, start, CB + 2 * W, 0)
        mask_here = lax.dynamic_slice_in_dim(present, start, CB, 0).astype(jnp.float32)
        applied = stack_offsets(s_ext, z_ext[W:W + CB], image_terms(W), False, CB).astype(jnp.bfloat16)
        return (mask_here * (centre - stack_offsets(z_ext, applied, defect_terms(W), True, CB))).astype(jnp.bfloat16)
    defect_all = lax.map(first_pass, group_ids).reshape(NB, 2 * W + 1, B, B)
    squares_sum = jnp.sum(jnp.square(defect_all.astype(jnp.float32)))
    defect_norm = jnp.sqrt(squares_sum / (NB * B))
    d_pad = jnp.pad(defect_all, pad_spec)

    def second_pass(group):
        start = (group * CB).astype(jnp.int32)
        d_ext = lax.dynamic_slice_in_dim(d_pad, start, CB + 2 * W, 0)
        z_ext = lax.dynamic_slice_in_dim(z_pad, start, CB + 2 * W, 0)
        mask_here = lax.dynamic_slice_in_dim(present, start, CB, 0).astype(jnp.float32)
        d_own = d_ext[W:W + CB]
        square = (mask_here * stack_offsets(d_ext, d_own, near_terms(W), False, CB)).astype(jnp.bfloat16)
        first_part = stack_offsets(z_ext, d_own, near_terms(W), False, CB)
        second_part = stack_offsets(z_ext, square, near_terms(W), False, CB)
        z_own = z_ext[W:W + CB].astype(jnp.float32)
        return (mask_here * (z_own + 0.5 * first_part + 0.375 * second_part)).astype(jnp.bfloat16)
    refined = lax.map(second_pass, group_ids).reshape(NB, 2 * W + 1, B, B)
    return (refined, defect_norm)
```

```python
import functools

import jax
import jax.numpy as jnp
from jax import lax
from jax.experimental import pallas as pl
from jax.experimental.pallas import tpu as pltpu
from jax.sharding import PartitionSpec as P

B = 128
W = 2
OFFS = 2 * W + 1
COLS = 4
SUP = 2 * B
BAND = 3 * SUP
PLANE = 8
MESH = pl.DeviceIdType.MESH


def dot(left, right):
    return jnp.dot(left, right, preferred_element_type=jnp.float32)


def kernel(
    n_grp,
    n_slab,
    margin,
    factor,
    pat,
    out,
    norm,
    sb,
    zb,
    zt,
    pb,
    db,
    eb,
    tu,
    td,
    ts,
    acc,
    acc2,
    part_a,
    part_b,
    load_sem,
    send_sem,
    recv_sem,
    sum_send,
    sum_recv,
):
    grp = lax.axis_index("grp")
    slab = lax.axis_index("slab")
    count = n_grp * n_slab
    n_plane = n_grp * PLANE
    n_z = n_slab // PLANE
    here = grp * n_slab + slab

    def device(flat):
        return (lax.div(flat, n_slab), lax.rem(flat, n_slab))

    right = device(lax.rem(here + 1, count))
    left = device(lax.rem(here + count - 1, count))
    z_here = lax.div(slab, PLANE)
    in_plane = grp * PLANE + lax.rem(slab, PLANE)

    def plane_device(index):
        return (lax.div(index, PLANE), z_here * PLANE + lax.rem(index, PLANE))

    def z_device(index):
        return (grp, index * PLANE + lax.rem(slab, PLANE))

    loads = []
    for column in (0, 3, 1, 2):
        for which, (source, band) in enumerate(((margin, sb), (factor, zb))):
            half = column % 2
            copy = pltpu.make_async_copy(
                source.at[column],
                band.at[1 + column // 2, pl.ds(half * B, OFFS * B), pl.ds(half * B, B)],
                load_sem.at[2 * column + which],
            )
            copy.start()
            loads.append((column, which, copy))

    barrier = pltpu.get_barrier_semaphore()
    for neighbour in (left, right):
        pl.semaphore_signal(barrier, inc=1, device_id=neighbour, device_id_type=MESH)

    def greet_plane(step, carry):
        peer = plane_device(lax.rem(in_plane + step, n_plane))
        pl.semaphore_signal(barrier, inc=1, device_id=peer, device_id_type=MESH)
        return carry

    def greet_z(step, carry):
        peer = z_device(lax.rem(z_here + step, n_z))
        pl.semaphore_signal(barrier, inc=1, device_id=peer, device_id_type=MESH)
        return carry

    lax.fori_loop(1, n_z, greet_z, 0)
    lax.fori_loop(1, n_plane, greet_plane, 0)

    blank = jnp.zeros((B, B), jnp.bfloat16)
    for band in (sb, zb, db):
        for index in range(4):
            band[index, pl.ds(5 * B, B), pl.ds(0, B)] = blank
            band[index, pl.ds(0, B), pl.ds(B, B)] = blank
    for index in range(2):
        eb[index, pl.ds(5 * B, B), pl.ds(0, B)] = blank
        eb[index, pl.ds(0, B), pl.ds(B, B)] = blank

    def present(column, offset):
        return pat[column, offset].astype(jnp.float32)

    first = (slab > 0).astype(jnp.float32)
    last = (slab < n_slab - 1).astype(jnp.float32)

    for column, which, copy in loads:
        copy.wait()
        half = column % 2
        band = (sb, zb)[which]
        for offset in range(OFFS):
            scale = present(column, offset)
            row = column + offset - W
            if which == 1 and row < 0:
                scale = scale * first
            if which == 1 and row >= COLS:
                scale = scale * last
            where = (1 + column // 2, pl.ds((half + offset) * B, B), pl.ds(half * B, B))
            band[where] = (band[where].astype(jnp.float32) * scale).astype(jnp.bfloat16)

    pl.semaphore_wait(barrier, 2 + (n_plane - 1) + (n_z - 1))

    started = []

    def send(source, target, peer):
        index = len(started)
        copy = pltpu.make_async_remote_copy(
            src_ref=source,
            dst_ref=target,
            send_sem=send_sem.at[index],
            recv_sem=recv_sem.at[index],
            device_id=peer,
            device_id_type=MESH,
        )
        copy.start()
        started.append(copy)
        return copy

    def send_band(band):
        to_left = [
            send(
                band.at[1, pl.ds(first_row, rows), pl.ds(half * B, B)],
                band.at[3, pl.ds(first_row, rows), pl.ds(half * B, B)],
                left,
            )
            for half, first_row, rows in ((0, 0, 4 * B), (1, B, 3 * B))
        ]
        to_right = [
            send(
                band.at[2, pl.ds(first_row, rows), pl.ds(half * B, B)],
                band.at[0, pl.ds(first_row, rows), pl.ds(half * B, B)],
                right,
            )
            for half, first_row, rows in ((0, 2 * B, 3 * B), (1, 2 * B, 4 * B))
        ]
        return to_left + to_right

    s_halo = send_band(sb)
    z_halo = send_band(zb)

    def flip(inner, outer):
        value = zb[outer + 1, pl.ds((inner - outer + 1) * SUP, SUP), :]
        zt[inner + 1, pl.ds((outer - inner + 1) * SUP, SUP), :] = value.T

    for outer in (0, 1):
        for inner in (outer - 1, outer, outer + 1):
            flip(inner, outer)

    def upper(column):
        return dot(zt[column, pl.ds(2 * SUP, SUP), :], sb[column + 1, pl.ds(0, SUP), :])

    def lower(column):
        return dot(zt[column + 2, pl.ds(0, SUP), :], sb[column + 1, pl.ds(2 * SUP, SUP), :])

    ts[0] = lower(0).astype(jnp.bfloat16)
    ts[1] = upper(1).astype(jnp.bfloat16)
    t_halo = [send(ts.at[0], td.at[1], left), send(ts.at[1], tu.at[0], right)]
    tu[1] = upper(0).astype(jnp.bfloat16)
    td[0] = lower(1).astype(jnp.bfloat16)

    def near(bands, values, own, row, inners):
        total = None
        for inner in inners:
            if abs(row - inner) > 1:
                continue
            term = dot(
                bands[own + inner, pl.ds((row - inner + 1) * SUP, SUP), :],
                values[pl.ds(inner * SUP, SUP), :],
            )
            total = term if total is None else total + term
        return total

    local = {0: (1, 2), 1: (0, 1)}
    halo = {0: 0, 1: 2}

    for own in (0, 1):
        for row in range(3):
            acc[own, pl.ds(row * SUP, SUP), :] = near(sb, zb.at[own + 1], own, row, local[own])

    for copy in s_halo:
        copy.wait_recv()
    for own in (0, 1):
        for row in range(3):
            where = (own, pl.ds(row * SUP, SUP), slice(None))
            total = acc[where]
            extra = near(sb, zb.at[own + 1], own, row, (halo[own],))
            if extra is not None:
                total = total + extra
            pb[where] = total.astype(jnp.bfloat16)

    eye = (
        lax.broadcasted_iota(jnp.int32, (B, B), 0) == lax.broadcasted_iota(jnp.int32, (B, B), 1)
    ).astype(jnp.float32)

    def blocks_of(own, row):
        for r in range(2):
            for c in range(2):
                offset = 2 * row + r - c
                if 0 <= offset < OFFS:
                    yield r, c, 2 * own + c, offset

    squares = jnp.zeros((8, B), jnp.float32)

    def defect(own, row, squares):
        total = near(zt, pb.at[own], own, row, (0, 1, 2))
        if row == 0:
            total = total + dot(tu[own], zb[own + 1, pl.ds(0, SUP), :])
        if row == 2:
            total = total + dot(td[own], zb[own + 1, pl.ds(2 * SUP, SUP), :])
        for r, c, column, offset in blocks_of(own, row):
            block = -total[r * B : (r + 1) * B, c * B : (c + 1) * B]
            if offset == W:
                block = eye + block
            block = (block * present(column, offset)).astype(jnp.bfloat16)
            db[own + 1, pl.ds((2 * row + r) * B, B), pl.ds(c * B, B)] = block
            wide = block.astype(jnp.float32)
            squares = squares + jnp.sum((wide * wide).reshape(B // 8, 8, B), axis=0)
        return squares

    for own, rows in ((0, (1, 2)), (1, (0, 1))):
        for row in rows:
            squares = defect(own, row, squares)

    for copy in z_halo + t_halo:
        copy.wait_recv()
    flip(-1, -1)
    flip(0, -1)
    flip(1, 2)
    flip(2, 2)
    squares = defect(0, 0, squares)
    squares = defect(1, 2, squares)

    d_halo = send_band(db)

    part_a[in_plane] = jnp.sum(squares, axis=0, keepdims=True)

    def sum_copy(buffer, slot, stage, peer):
        return pltpu.make_async_remote_copy(
            src_ref=buffer.at[slot],
            dst_ref=buffer.at[slot],
            send_sem=sum_send.at[stage],
            recv_sem=sum_recv.at[stage],
            device_id=peer,
            device_id_type=MESH,
        )

    def send_plane(step, carry):
        sum_copy(part_a, in_plane, 0, plane_device(lax.rem(in_plane + step, n_plane))).start()
        return carry

    def send_z(step, carry):
        sum_copy(part_b, z_here, 1, z_device(lax.rem(z_here + step, n_z))).start()
        return carry

    def all_of(buffer, rows, sem):
        return pltpu.make_async_copy(buffer.at[pl.ds(0, rows)], buffer.at[pl.ds(0, rows)], sem)

    lax.fori_loop(1, n_plane, send_plane, 0)

    for own in (0, 1):
        for row in range(3):
            where = (own, pl.ds(row * SUP, SUP), slice(None))
            acc[where] = near(zb, db.at[own + 1], own, row, (0, 1, 2))
            acc2[where] = near(db, db.at[own + 1], own, row, local[own])

    all_of(part_a, n_plane - 1, sum_recv.at[0]).wait()
    part_b[z_here] = jnp.sum(part_a[...], axis=0)
    lax.fori_loop(1, n_z, send_z, 0)

    for copy in d_halo:
        copy.wait_recv()
    for own in (0, 1):
        for row in range(3):
            total = acc2[own, pl.ds(row * SUP, SUP), :]
            extra = near(db, db.at[own + 1], own, row, (halo[own],))
            if extra is not None:
                total = total + extra
            for r, c, column, offset in blocks_of(own, row):
                block = total[r * B : (r + 1) * B, c * B : (c + 1) * B]
                block = (block * present(column, offset)).astype(jnp.bfloat16)
                eb[own, pl.ds((2 * row + r) * B, B), pl.ds(c * B, B)] = block

    for own in (0, 1):
        for row in range(3):
            total = 0.375 * near(zb, eb.at[own], own, row, (0, 1, 2))
            total = total + 0.5 * acc[own, pl.ds(row * SUP, SUP), :]
            for r, c, column, offset in blocks_of(own, row):
                block = total[r * B : (r + 1) * B, c * B : (c + 1) * B]
                base = zb[own + 1, pl.ds((2 * row + r) * B, B), pl.ds(c * B, B)]
                block = (block + base.astype(jnp.float32)) * present(column, offset)
                out[column, offset] = block.astype(jnp.bfloat16)

    all_of(part_b, n_z - 1, sum_recv.at[1]).wait()
    total = jnp.sum(jnp.sum(part_b[...], axis=0), axis=1, keepdims=True)
    norm[...] = jnp.sqrt(total / (count * COLS * B))

    for copy in started:
        copy.wait_send()
    all_of(part_a, n_plane - 1, sum_send.at[0]).wait()
    all_of(part_b, n_z - 1, sum_send.at[1]).wait()


def solution(mesh):
    n_grp, n_slab = mesh.shape["grp"], mesh.shape["slab"]
    n_plane, n_z = n_grp * PLANE, n_slab // PLANE

    def step(margin, factor, pattern):
        bands = pltpu.VMEM((4, BAND, SUP), jnp.bfloat16)
        pairs = pltpu.VMEM((2, BAND, SUP), jnp.bfloat16)
        wide = pltpu.VMEM((2, BAND, SUP), jnp.float32)
        corner = pltpu.VMEM((2, SUP, SUP), jnp.bfloat16)
        refined, norm = pl.pallas_call(
            functools.partial(kernel, n_grp, n_slab),
            out_shape=(
                jax.ShapeDtypeStruct((COLS, OFFS, B, B), jnp.bfloat16),
                jax.ShapeDtypeStruct((1, 1), jnp.float32),
            ),
            in_specs=[
                pl.BlockSpec(memory_space=pl.ANY),
                pl.BlockSpec(memory_space=pl.ANY),
                pl.BlockSpec(memory_space=pltpu.SMEM),
            ],
            out_specs=(
                pl.BlockSpec(memory_space=pltpu.VMEM),
                pl.BlockSpec(memory_space=pltpu.VMEM),
            ),
            scratch_shapes=[
                bands,
                bands,
                bands,
                pairs,
                bands,
                pairs,
                corner,
                corner,
                corner,
                wide,
                wide,
                pltpu.VMEM((n_plane, 1, B), jnp.float32),
                pltpu.VMEM((n_z, 1, B), jnp.float32),
                pltpu.SemaphoreType.DMA((2 * COLS,)),
                pltpu.SemaphoreType.DMA((14,)),
                pltpu.SemaphoreType.DMA((14,)),
                pltpu.SemaphoreType.DMA((2,)),
                pltpu.SemaphoreType.DMA((2,)),
            ],
            compiler_params=pltpu.CompilerParams(collective_id=0, has_side_effects=True),
        )(
            margin.reshape(COLS, OFFS * B, B),
            factor.reshape(COLS, OFFS * B, B),
            pattern,
        )
        return refined, norm.reshape(())

    return jax.shard_map(
        step,
        mesh=mesh,
        in_specs=(
            P(("grp", "slab"), None, None, None),
            P(("grp", "slab"), None, None, None),
            P(("grp", "slab"), None),
        ),
        out_specs=(P(("grp", "slab"), None, None, None), P()),
        check_vma=False,
    )
```

```python
import functools

import jax
import jax.numpy as jnp
from jax import lax
from jax.experimental import pallas as pl
from jax.experimental.pallas import tpu as pltpu
from jax.sharding import PartitionSpec as P

B = 128
W = 2
OFFS = 2 * W + 1
COLS = 4
SUP = 2 * B
BAND = 3 * SUP
PLANE = 8
COPIES = 26
MESH = pl.DeviceIdType.MESH


def dot(left, right):
    return jnp.dot(left, right, preferred_element_type=jnp.float32)


def kernel(
    n_grp,
    n_slab,
    margin,
    factor,
    pat,
    out,
    norm,
    sb,
    zb,
    zt,
    pb,
    db,
    eb,
    tu,
    td,
    ts,
    acc,
    acc2,
    part_a,
    part_b,
    load_sem,
    send_sem,
    recv_sem,
    sum_send,
    sum_recv,
    known,
):
    grp = lax.axis_index("grp")
    slab = lax.axis_index("slab")
    count = n_grp * n_slab
    n_plane = n_grp * PLANE
    n_z = n_slab // PLANE
    here = grp * n_slab + slab

    def device(flat):
        return (lax.div(flat, n_slab), lax.rem(flat, n_slab))

    right = device(lax.rem(here + 1, count))
    left = device(lax.rem(here + count - 1, count))
    z_here = lax.div(slab, PLANE)
    in_plane = grp * PLANE + lax.rem(slab, PLANE)

    def plane_device(index):
        return (lax.div(index, PLANE), z_here * PLANE + lax.rem(index, PLANE))

    def z_device(index):
        return (grp, index * PLANE + lax.rem(slab, PLANE))

    loads = {}
    for which, (source, band) in enumerate(((margin, sb), (factor, zb))):
        for column in range(COLS):
            half = column % 2
            copy = pltpu.make_async_copy(
                source.at[column],
                band.at[1 + column // 2, pl.ds(half * B, OFFS * B), pl.ds(half * B, B)],
                load_sem.at[2 * column + which],
            )
            copy.start()
            loads[which, column] = copy

    row_here, core = lax.div(lax.rem(slab, PLANE), 2), lax.rem(slab, 2)
    n_row = PLANE // 2

    def along_x(step):
        return (lax.rem(grp + n_grp + step, n_grp), slab)

    def along_y(step):
        return (grp, z_here * PLANE + lax.rem(row_here + n_row + step, n_row) * 2 + core)

    def along_z(step):
        return (grp, lax.rem(slab + n_slab + step * PLANE, n_slab))

    mate = (grp, slab + 1 - 2 * core)

    def signal(sem, *peers):
        for peer in peers:
            pl.semaphore_signal(sem, inc=1, device_id=peer, device_id_type=MESH)

    barrier = pltpu.get_barrier_semaphore()
    near_by = (left, right, along_y(1), along_y(-1), along_x(1), along_x(-1), along_z(1), along_z(-1))
    signal(barrier, *near_by)

    blank = jnp.zeros((B, B), jnp.bfloat16)
    for band in (sb, zb, db):
        for index in range(4):
            band[index, pl.ds(5 * B, B), pl.ds(0, B)] = blank
            band[index, pl.ds(0, B), pl.ds(B, B)] = blank
    for index in range(2):
        eb[index, pl.ds(5 * B, B), pl.ds(0, B)] = blank
        eb[index, pl.ds(0, B), pl.ds(B, B)] = blank

    def present(column, offset):
        return pat[column, offset].astype(jnp.float32)

    first = (slab > 0).astype(jnp.float32)
    last = (slab < n_slab - 1).astype(jnp.float32)

    def place(index, half, block, blocks=1):
        return (index, pl.ds(block * B, blocks * B), pl.ds(half * B, B))

    def scale_block(band, where, scale):
        factors = jnp.full((B, B), scale, jnp.float32).astype(jnp.bfloat16)
        band[where] = band[where] * factors

    pl.semaphore_wait(barrier, len(near_by))

    started = []

    def send(source, target, peer):
        index = len(started)
        copy = pltpu.make_async_remote_copy(
            src_ref=source,
            dst_ref=target,
            send_sem=send_sem.at[index],
            recv_sem=recv_sem.at[index],
            device_id=peer,
            device_id_type=MESH,
        )
        copy.start()
        started.append(copy)
        return copy

    def send_band(band):
        to_left = [
            send(
                band.at[1, pl.ds(first_row, rows), pl.ds(half * B, B)],
                band.at[3, pl.ds(first_row, rows), pl.ds(half * B, B)],
                left,
            )
            for half, first_row, rows in ((0, 0, 4 * B), (1, B, 3 * B))
        ]
        to_right = [
            send(
                band.at[2, pl.ds(first_row, rows), pl.ds(half * B, B)],
                band.at[0, pl.ds(first_row, rows), pl.ds(half * B, B)],
                right,
            )
            for half, first_row, rows in ((0, 2 * B, 3 * B), (1, 2 * B, 4 * B))
        ]
        return to_left + to_right

    raw_left, raw_right = ((0, 0, 3), (1, 0, 1), (1, 2, 1)), ((2, 2, 1), (2, 4, 1), (3, 2, 3))
    own_left, own_right = ((0, 3), (1, 1)), ((2, 3), (3, 1))

    def send_raw(source, band):
        copies = []
        for index in range(3):
            for peer, target, pieces in ((left, 3, raw_left), (right, 0, raw_right)):
                column, offset, offsets = pieces[index]
                half = column % 2
                copies.append(
                    send(
                        source.at[column, pl.ds(offset * B, offsets * B), :],
                        band.at[place(target, half, offset + half, offsets)],
                        peer,
                    )
                )
        return copies

    def send_own(band):
        copies = []
        for index in range(2):
            for peer, target, pieces in ((left, 3, own_left), (right, 0, own_right)):
                column, offset = pieces[index]
                half = column % 2
                copies.append(
                    send(
                        band.at[place(1 + column // 2, half, offset + half)],
                        band.at[place(target, half, offset + half)],
                        peer,
                    )
                )
        return copies

    s_halo = send_raw(margin, sb)
    z_halo = send_raw(factor, zb)
    signal(known.at[0], along_y(1), along_y(-1))
    signal(known.at[3], along_z(1), along_z(-1))

    for which, (band, halo_copies) in enumerate(((sb, s_halo), (zb, z_halo))):
        for column in range(COLS):
            loads[which, column].wait()
        for column in range(COLS):
            half = column % 2
            for offset in range(OFFS):
                if offset == W:
                    continue
                scale = present(column, offset)
                row = column + offset - W
                if which == 1 and row < 0:
                    scale = scale * first
                if which == 1 and row >= COLS:
                    scale = scale * last
                scale_block(band, place(1 + column // 2, half, half + offset), scale)
        halo_copies.extend(send_own(band))

    def mask_halo(band, low, high):
        for half, block, column, offset in ((0, 4, 0, 0), (1, 4, 0, 1), (1, 5, 1, 0)):
            scale_block(band, place(0, half, block), present(column, offset) * low)
        for half, block, column, offset in ((0, 0, 2, 4), (0, 1, 3, 3), (1, 1, 3, 4)):
            scale_block(band, place(3, half, block), present(column, offset) * high)

    pl.semaphore_wait(known.at[0], 2)
    signal(known.at[1], mate)
    pl.semaphore_wait(known.at[3], 2)
    signal(known.at[4], along_z(2), along_z(-2))

    def flip(inner, outer):
        value = zb[outer + 1, pl.ds((inner - outer + 1) * SUP, SUP), :]
        zt[inner + 1, pl.ds((outer - inner + 1) * SUP, SUP), :] = value.T

    for outer in (0, 1):
        for inner in (outer - 1, outer, outer + 1):
            flip(inner, outer)

    def upper(column):
        return dot(zt[column, pl.ds(2 * SUP, SUP), :], sb[column + 1, pl.ds(0, SUP), :])

    def lower(column):
        return dot(zt[column + 2, pl.ds(0, SUP), :], sb[column + 1, pl.ds(2 * SUP, SUP), :])

    ts[0] = lower(0).astype(jnp.bfloat16)
    ts[1] = upper(1).astype(jnp.bfloat16)
    t_halo = [send(ts.at[0], td.at[1], left), send(ts.at[1], tu.at[0], right)]
    tu[1] = upper(0).astype(jnp.bfloat16)
    td[0] = lower(1).astype(jnp.bfloat16)

    def near(bands, values, own, row, inners):
        total = None
        for inner in inners:
            if abs(row - inner) > 1:
                continue
            term = dot(
                bands[own + inner, pl.ds((row - inner + 1) * SUP, SUP), :],
                values[pl.ds(inner * SUP, SUP), :],
            )
            total = term if total is None else total + term
        return total

    local = {0: (1, 2), 1: (0, 1)}
    halo = {0: 0, 1: 2}

    for own in (0, 1):
        for row in range(3):
            acc[own, pl.ds(row * SUP, SUP), :] = near(sb, zb.at[own + 1], own, row, local[own])

    pl.semaphore_wait(known.at[1], 1)
    signal(known.at[2], along_x(1), along_x(-1))
    pl.semaphore_wait(known.at[4], 2)
    signal(known.at[5], along_z(4), along_z(-4))

    for copy in s_halo:
        copy.wait_recv()
    mask_halo(sb, 1.0, 1.0)
    for own in (0, 1):
        for row in range(3):
            where = (own, pl.ds(row * SUP, SUP), slice(None))
            total = acc[where]
            extra = near(sb, zb.at[own + 1], own, row, (halo[own],))
            if extra is not None:
                total = total + extra
            pb[where] = total.astype(jnp.bfloat16)

    eye = (
        lax.broadcasted_iota(jnp.int32, (B, B), 0) == lax.broadcasted_iota(jnp.int32, (B, B), 1)
    ).astype(jnp.float32)

    def blocks_of(own, row):
        for r in range(2):
            for c in range(2):
                offset = 2 * row + r - c
                if 0 <= offset < OFFS:
                    yield r, c, 2 * own + c, offset

    squares = jnp.zeros((8, B), jnp.float32)

    def defect(own, row, total, squares):
        for r, c, column, offset in blocks_of(own, row):
            block = -total[r * B : (r + 1) * B, c * B : (c + 1) * B]
            if offset == W:
                block = eye + block
            else:
                block = block * present(column, offset)
            block = block.astype(jnp.bfloat16)
            db[own + 1, pl.ds((2 * row + r) * B, B), pl.ds(c * B, B)] = block
            wide = block.astype(jnp.float32)
            squares = squares + jnp.sum((wide * wide).reshape(B // 8, 8, B), axis=0)
        return squares

    def outer(own, row):
        corner = (tu, td)[row // 2]
        return dot(corner[own], zb[own + 1, pl.ds(row * SUP, SUP), :])

    for own, rows in ((0, (1, 2)), (1, (0, 1))):
        for row in rows:
            total = near(zt, pb.at[own], own, row, (0, 1, 2))
            if row != 1:
                total = total + outer(own, row)
            squares = defect(own, row, total, squares)

    pl.semaphore_wait(known.at[2], 2)
    signal(known.at[6], along_x(2))
    pl.semaphore_wait(known.at[5], 2)

    for copy in z_halo:
        copy.wait_recv()
    mask_halo(zb, first, last)
    flip(-1, -1)
    flip(0, -1)
    flip(1, 2)
    flip(2, 2)
    edges = ((0, 0), (1, 2))
    for own, row in edges:
        acc[own, pl.ds(row * SUP, SUP), :] = near(zt, pb.at[own], own, row, (0, 1, 2))
    for copy in t_halo:
        copy.wait_recv()
    for own, row in edges:
        total = acc[own, pl.ds(row * SUP, SUP), :] + outer(own, row)
        squares = defect(own, row, total, squares)

    part_a[in_plane] = jnp.sum(squares, axis=0, keepdims=True)
    pl.semaphore_wait(known.at[6], 1)

    def sum_copy(buffer, slot, stage, peer):
        return pltpu.make_async_remote_copy(
            src_ref=buffer.at[slot],
            dst_ref=buffer.at[slot],
            send_sem=sum_send.at[stage],
            recv_sem=sum_recv.at[stage],
            device_id=peer,
            device_id_type=MESH,
        )

    def send_plane(step, carry):
        sum_copy(part_a, in_plane, 0, plane_device(lax.rem(in_plane + step, n_plane))).start()
        return carry

    def send_z(step, carry):
        sum_copy(part_b, z_here, 1, z_device(lax.rem(z_here + step, n_z))).start()
        return carry

    def all_of(buffer, rows, sem):
        return pltpu.make_async_copy(buffer.at[pl.ds(0, rows)], buffer.at[pl.ds(0, rows)], sem)

    lax.fori_loop(1, n_plane, send_plane, 0)
    d_halo = send_band(db)

    for own in (0, 1):
        for row in range(3):
            where = (own, pl.ds(row * SUP, SUP), slice(None))
            acc[where] = near(zb, db.at[own + 1], own, row, (0, 1, 2))
            acc2[where] = near(db, db.at[own + 1], own, row, local[own])

    all_of(part_a, n_plane - 1, sum_recv.at[0]).wait()
    part_b[z_here] = jnp.sum(part_a[...], axis=0)
    lax.fori_loop(1, n_z, send_z, 0)

    for copy in d_halo:
        copy.wait_recv()
    for own in (0, 1):
        for row in range(3):
            total = acc2[own, pl.ds(row * SUP, SUP), :]
            extra = near(db, db.at[own + 1], own, row, (halo[own],))
            if extra is not None:
                total = total + extra
            for r, c, column, offset in blocks_of(own, row):
                block = total[r * B : (r + 1) * B, c * B : (c + 1) * B]
                block = (block * present(column, offset)).astype(jnp.bfloat16)
                eb[own, pl.ds((2 * row + r) * B, B), pl.ds(c * B, B)] = block

    for own in (0, 1):
        for row in range(3):
            total = 0.375 * near(zb, eb.at[own], own, row, (0, 1, 2))
            total = total + 0.5 * acc[own, pl.ds(row * SUP, SUP), :]
            for r, c, column, offset in blocks_of(own, row):
                block = total[r * B : (r + 1) * B, c * B : (c + 1) * B]
                base = zb[own + 1, pl.ds((2 * row + r) * B, B), pl.ds(c * B, B)]
                block = (block + base.astype(jnp.float32)) * present(column, offset)
                out[column, offset] = block.astype(jnp.bfloat16)

    all_of(part_b, n_z - 1, sum_recv.at[1]).wait()
    total = jnp.sum(jnp.sum(part_b[...], axis=0), axis=1, keepdims=True)
    norm[...] = jnp.sqrt(total / (count * COLS * B))

    for copy in started:
        copy.wait_send()
    all_of(part_a, n_plane - 1, sum_send.at[0]).wait()
    all_of(part_b, n_z - 1, sum_send.at[1]).wait()


def in_hbm(array):
    return pltpu.with_memory_space_constraint(array, pltpu.HBM)


def solution(mesh):
    n_grp, n_slab = mesh.shape["grp"], mesh.shape["slab"]
    n_plane, n_z = n_grp * PLANE, n_slab // PLANE

    def step(margin, factor, pattern):
        bands = pltpu.VMEM((4, BAND, SUP), jnp.bfloat16)
        pairs = pltpu.VMEM((2, BAND, SUP), jnp.bfloat16)
        wide = pltpu.VMEM((2, BAND, SUP), jnp.float32)
        corner = pltpu.VMEM((2, SUP, SUP), jnp.bfloat16)
        refined, norm = pl.pallas_call(
            functools.partial(kernel, n_grp, n_slab),
            out_shape=(
                jax.ShapeDtypeStruct((COLS, OFFS, B, B), jnp.bfloat16),
                jax.ShapeDtypeStruct((1, 1), jnp.float32),
            ),
            in_specs=[
                pl.BlockSpec(memory_space=pltpu.HBM),
                pl.BlockSpec(memory_space=pltpu.HBM),
                pl.BlockSpec(memory_space=pltpu.SMEM),
            ],
            out_specs=(
                pl.BlockSpec(memory_space=pltpu.VMEM),
                pl.BlockSpec(memory_space=pltpu.VMEM),
            ),
            scratch_shapes=[
                bands,
                bands,
                bands,
                pairs,
                bands,
                pairs,
                corner,
                corner,
                corner,
                wide,
                wide,
                pltpu.VMEM((n_plane, 1, B), jnp.float32),
                pltpu.VMEM((n_z, 1, B), jnp.float32),
                pltpu.SemaphoreType.DMA((2 * COLS,)),
                pltpu.SemaphoreType.DMA((COPIES,)),
                pltpu.SemaphoreType.DMA((COPIES,)),
                pltpu.SemaphoreType.DMA((2,)),
                pltpu.SemaphoreType.DMA((2,)),
                pltpu.SemaphoreType.REGULAR((7,)),
            ],
            compiler_params=pltpu.CompilerParams(
                collective_id=0, has_side_effects=True, vmem_limit_bytes=24 << 20
            ),
        )(
            in_hbm(margin.reshape(COLS, OFFS * B, B)),
            in_hbm(factor.reshape(COLS, OFFS * B, B)),
            in_hbm(pattern),
        )
        return refined, norm.reshape(())

    return jax.shard_map(
        step,
        mesh=mesh,
        in_specs=(
            P(("grp", "slab"), None, None, None),
            P(("grp", "slab"), None, None, None),
            P(("grp", "slab"), None),
        ),
        out_specs=(P(("grp", "slab"), None, None, None), P()),
        check_vma=False,
    )
```

```python
import functools

import jax
import jax.numpy as jnp
from jax import lax
from jax.experimental import pallas as pl
from jax.experimental.pallas import tpu as pltpu
from jax.sharding import PartitionSpec as P

B = 128
W = 2
OFFS = 2 * W + 1
COLS = 4
SUP = 2 * B
BAND = 3 * SUP
PLANE = 8
COPIES = 28
MESH = pl.DeviceIdType.MESH


def dot(left, right):
    return jnp.dot(left, right, preferred_element_type=jnp.float32)


def kernel(
    n_grp,
    n_slab,
    margin,
    factor,
    pattern,
    out,
    norm,
    sb,
    zb,
    zt,
    pb,
    db,
    eb,
    tu,
    td,
    ts,
    acc,
    acc2,
    part_a,
    part_b,
    load_sem,
    send_sem,
    recv_sem,
    sum_send,
    sum_recv,
    known,
    pat,
    pat_sem,
):
    grp = lax.axis_index("grp")
    slab = lax.axis_index("slab")
    count = n_grp * n_slab
    n_plane = n_grp * PLANE
    n_z = n_slab // PLANE
    here = grp * n_slab + slab

    def device(flat):
        return (lax.div(flat, n_slab), lax.rem(flat, n_slab))

    right = device(lax.rem(here + 1, count))
    left = device(lax.rem(here + count - 1, count))
    z_here = lax.div(slab, PLANE)
    in_plane = grp * PLANE + lax.rem(slab, PLANE)

    row_here, core = lax.div(lax.rem(slab, PLANE), 2), lax.rem(slab, 2)
    n_row = PLANE // 2

    def along_x(step):
        return (lax.rem(grp + n_grp + step, n_grp), slab)

    def along_y(step):
        return (grp, z_here * PLANE + lax.rem(row_here + n_row + step, n_row) * 2 + core)

    def along_z(step):
        return (grp, lax.rem(slab + n_slab + step * PLANE, n_slab))

    mate = (grp, slab + 1 - 2 * core)

    def signal(sem, *peers):
        for peer in peers:
            pl.semaphore_signal(sem, inc=1, device_id=peer, device_id_type=MESH)

    barrier = pltpu.get_barrier_semaphore()
    near_by = (left, right, along_y(1), along_y(-1), along_x(1), along_x(-1), along_z(1), along_z(-1))
    signal(barrier, *near_by)

    pattern_copy = pltpu.make_async_copy(pattern, pat, pat_sem)
    pattern_copy.start()
    loads = {}
    for which, (source, band) in enumerate(((margin, sb), (factor, zb))):
        for column in range(COLS):
            half = column % 2
            copy = pltpu.make_async_copy(
                source.at[column],
                band.at[1 + column // 2, pl.ds(half * B, OFFS * B), pl.ds(half * B, B)],
                load_sem.at[2 * column + which],
            )
            copy.start()
            loads[which, column] = copy

    blank = jnp.zeros((B, B), jnp.bfloat16)
    for band in (sb, zb, db):
        for index in range(4):
            band[index, pl.ds(5 * B, B), pl.ds(0, B)] = blank
            band[index, pl.ds(0, B), pl.ds(B, B)] = blank
    for index in range(2):
        eb[index, pl.ds(5 * B, B), pl.ds(0, B)] = blank
        eb[index, pl.ds(0, B), pl.ds(B, B)] = blank

    inner_left, inner_right = slab > 0, slab < n_slab - 1

    @pl.when(jnp.logical_not(inner_left))
    def _():
        sb[0, pl.ds(SUP, 2 * SUP), :] = jnp.zeros((2 * SUP, SUP), jnp.bfloat16)
        zb[0, pl.ds(2 * SUP, SUP), :] = jnp.zeros((SUP, SUP), jnp.bfloat16)
        tu[0] = jnp.zeros((SUP, SUP), jnp.bfloat16)

    def present(column, offset):
        return pat[column, offset].astype(jnp.float32)

    first = inner_left.astype(jnp.float32)
    last = inner_right.astype(jnp.float32)

    def place(index, half, block, blocks=1):
        return (index, pl.ds(block * B, blocks * B), pl.ds(half * B, B))

    def scale_block(band, where, scale):
        factors = jnp.full((B, B), scale, jnp.float32).astype(jnp.bfloat16)
        band[where] = band[where] * factors

    pl.semaphore_wait(barrier, len(near_by))

    used = iter(range(COPIES))

    def remote(source, target, peer):
        index = next(used)
        return pltpu.make_async_remote_copy(
            src_ref=source,
            dst_ref=target,
            send_sem=send_sem.at[index],
            recv_sem=recv_sem.at[index],
            device_id=peer,
            device_id_type=MESH,
        )

    def all_start(copies):
        for copy in copies:
            copy.start()

    def all_arrived(copies):
        for copy in copies:
            copy.wait_recv()

    def all_sent(copies):
        for copy in copies:
            copy.wait_send()

    raw_left, raw_right = ((0, 0, 3), (1, 0, 1), (1, 2, 1)), ((3, 2, 3), (2, 2, 1), (2, 4, 1))
    raw_edge = ((2, 2, 1), (3, 2, 1))
    own_left, own_right = ((0, 3), (1, 1)), ((2, 3), (3, 1))

    def raw(source, band, pieces, target, peer):
        return [
            remote(
                source.at[column, pl.ds(offset * B, offsets * B), :],
                band.at[place(target, column % 2, offset + column % 2, offsets)],
                peer,
            )
            for column, offset, offsets in pieces
        ]

    def masked(band, pieces, target, peer):
        return [
            remote(
                band.at[place(1 + column // 2, column % 2, offset + column % 2)],
                band.at[place(target, column % 2, offset + column % 2)],
                peer,
            )
            for column, offset in pieces
        ]

    s_raw_left = raw(margin, sb, raw_left, 3, left)
    s_raw_right = raw(margin, sb, raw_right, 0, right)
    z_raw_left = raw(factor, zb, raw_left, 3, left)
    z_raw_right = raw(factor, zb, raw_right, 0, right)
    z_raw_edge = raw(factor, zb, raw_edge, 0, right)
    s_own_left, s_own_right = masked(sb, own_left, 3, left), masked(sb, own_right, 0, right)
    z_own_left, z_own_right = masked(zb, own_left, 3, left), masked(zb, own_right, 0, right)

    @pl.when(inner_right)
    def _():
        all_start(s_raw_right)

    @pl.when(jnp.logical_not(inner_right))
    def _():
        all_start(z_raw_edge)

    all_start(s_raw_left)

    @pl.when(inner_right)
    def _():
        all_start(z_raw_right)

    all_start(z_raw_left)
    signal(known.at[0], along_y(1), along_y(-1))
    signal(known.at[3], along_z(1), along_z(-1))
    pattern_copy.wait()

    def mask_own(which, band):
        for column in range(COLS):
            loads[which, column].wait()
        for column in range(COLS):
            half = column % 2
            for offset in range(OFFS):
                if offset == W:
                    continue
                scale = present(column, offset)
                row = column + offset - W
                if which == 1 and row < 0:
                    scale = scale * first
                if which == 1 and row >= COLS:
                    scale = scale * last
                scale_block(band, place(1 + column // 2, half, half + offset), scale)

    mask_own(0, sb)

    @pl.when(inner_right)
    def _():
        all_start(s_own_right)

    all_start(s_own_left)
    mask_own(1, zb)
    all_start(z_own_right + z_own_left)

    def mask_low(band):
        for half, block, column, offset in ((0, 4, 0, 0), (1, 4, 0, 1), (1, 5, 1, 0)):
            scale_block(band, place(0, half, block), present(column, offset))

    def mask_high(band, scale):
        for half, block, column, offset in ((0, 0, 2, 4), (0, 1, 3, 3), (1, 1, 3, 4)):
            scale_block(band, place(3, half, block), present(column, offset) * scale)

    pl.semaphore_wait(known.at[0], 2)
    signal(known.at[1], mate)
    pl.semaphore_wait(known.at[3], 2)
    signal(known.at[4], along_z(2), along_z(-2))

    def flip(inner, outer):
        value = zb[outer + 1, pl.ds((inner - outer + 1) * SUP, SUP), :]
        zt[inner + 1, pl.ds((outer - inner + 1) * SUP, SUP), :] = value.T

    for outer in (0, 1):
        for inner in (outer - 1, outer, outer + 1):
            flip(inner, outer)

    def upper(column):
        return dot(zt[column, pl.ds(2 * SUP, SUP), :], sb[column + 1, pl.ds(0, SUP), :])

    def lower(column):
        return dot(zt[column + 2, pl.ds(0, SUP), :], sb[column + 1, pl.ds(2 * SUP, SUP), :])

    ts[0] = lower(0).astype(jnp.bfloat16)
    ts[1] = upper(1).astype(jnp.bfloat16)
    t_left, t_right = [remote(ts.at[0], td.at[1], left)], [remote(ts.at[1], tu.at[0], right)]

    @pl.when(inner_right)
    def _():
        all_start(t_right)

    all_start(t_left)
    tu[1] = upper(0).astype(jnp.bfloat16)
    td[0] = lower(1).astype(jnp.bfloat16)

    def near(bands, values, own, row, inners):
        total = None
        for inner in inners:
            if abs(row - inner) > 1:
                continue
            term = dot(
                bands[own + inner, pl.ds((row - inner + 1) * SUP, SUP), :],
                values[pl.ds(inner * SUP, SUP), :],
            )
            total = term if total is None else total + term
        return total

    local = {0: (1, 2), 1: (0, 1)}
    halo = {0: 0, 1: 2}

    for own in (0, 1):
        for row in range(3):
            acc[own, pl.ds(row * SUP, SUP), :] = near(sb, zb.at[own + 1], own, row, local[own])

    pl.semaphore_wait(known.at[1], 1)
    signal(known.at[2], along_x(1), along_x(-1))
    pl.semaphore_wait(known.at[4], 2)
    signal(known.at[5], along_z(4), along_z(-4))

    @pl.when(inner_left)
    def _():
        all_arrived(s_raw_right + s_own_right)
        mask_low(sb)

    all_arrived(s_raw_left + s_own_left)
    mask_high(sb, 1.0)
    for own in (0, 1):
        for row in range(3):
            where = (own, pl.ds(row * SUP, SUP), slice(None))
            total = acc[where]
            extra = near(sb, zb.at[own + 1], own, row, (halo[own],))
            if extra is not None:
                total = total + extra
            pb[where] = total.astype(jnp.bfloat16)

    eye = (
        lax.broadcasted_iota(jnp.int32, (B, B), 0) == lax.broadcasted_iota(jnp.int32, (B, B), 1)
    ).astype(jnp.float32)

    def blocks_of(own, row):
        for r in range(2):
            for c in range(2):
                offset = 2 * row + r - c
                if 0 <= offset < OFFS:
                    yield r, c, 2 * own + c, offset

    squares = jnp.zeros((8, B), jnp.float32)

    def defect(own, row, total, squares):
        for r, c, column, offset in blocks_of(own, row):
            block = -total[r * B : (r + 1) * B, c * B : (c + 1) * B]
            if offset == W:
                block = eye + block
            else:
                block = block * present(column, offset)
            block = block.astype(jnp.bfloat16)
            db[own + 1, pl.ds((2 * row + r) * B, B), pl.ds(c * B, B)] = block
            wide = block.astype(jnp.float32)
            squares = squares + jnp.sum((wide * wide).reshape(B // 8, 8, B), axis=0)
        return squares

    def outer(own, row):
        corner = (tu, td)[row // 2]
        return dot(corner[own], zb[own + 1, pl.ds(row * SUP, SUP), :])

    for own, rows in ((0, (1, 2)), (1, (0, 1))):
        for row in rows:
            total = near(zt, pb.at[own], own, row, (0, 1, 2))
            if row != 1:
                total = total + outer(own, row)
            squares = defect(own, row, total, squares)

    pl.semaphore_wait(known.at[2], 2)
    signal(known.at[6], along_x(2))
    pl.semaphore_wait(known.at[5], 2)

    @pl.when(inner_left)
    def _():
        all_arrived(z_raw_right)
        mask_low(zb)

    @pl.when(jnp.logical_not(inner_left))
    def _():
        all_arrived(z_raw_edge)

    all_arrived(z_own_right + z_raw_left + z_own_left)
    mask_high(zb, last)
    flip(-1, -1)
    flip(0, -1)
    flip(1, 2)
    flip(2, 2)
    edges = ((0, 0), (1, 2))
    for own, row in edges:
        acc[own, pl.ds(row * SUP, SUP), :] = near(zt, pb.at[own], own, row, (0, 1, 2))
    @pl.when(inner_left)
    def _():
        all_arrived(t_right)

    all_arrived(t_left)
    for own, row in edges:
        total = acc[own, pl.ds(row * SUP, SUP), :] + outer(own, row)
        squares = defect(own, row, total, squares)

    part_a[in_plane] = jnp.sum(squares, axis=0, keepdims=True)
    pl.semaphore_wait(known.at[6], 1)

    def sum_copy(buffer, slot, stage, peer):
        return pltpu.make_async_remote_copy(
            src_ref=buffer.at[slot],
            dst_ref=buffer.at[slot],
            send_sem=sum_send.at[stage],
            recv_sem=sum_recv.at[stage],
            device_id=peer,
            device_id_type=MESH,
        )

    def hops(step, size):
        return min(step, size - step)

    plane_steps = sorted(
        ((x, y, c) for x in range(n_grp) for y in range(n_row) for c in range(2) if x or y or c),
        key=lambda step: -hops(step[0], n_grp) - hops(step[1], n_row),
    )
    z_steps = sorted(range(1, n_z), key=lambda step: -hops(step, n_z))

    def all_of(buffer, rows, sem):
        return pltpu.make_async_copy(buffer.at[pl.ds(0, rows)], buffer.at[pl.ds(0, rows)], sem)

    x_of = [lax.rem(grp + step, n_grp) for step in range(n_grp)]
    y_of = [z_here * PLANE + 2 * lax.rem(row_here + step, n_row) for step in range(n_row)]
    core_of = (core, 1 - core)
    for x, y, c in plane_steps:
        sum_copy(part_a, in_plane, 0, (x_of[x], y_of[y] + core_of[c])).start()
    d_halo = [
        remote(
            db.at[index, pl.ds(first_row, rows), pl.ds(half * B, B)],
            db.at[target, pl.ds(first_row, rows), pl.ds(half * B, B)],
            peer,
        )
        for index, target, peer, half, first_row, rows in (
            (1, 3, left, 0, 0, 4 * B),
            (2, 0, right, 1, 2 * B, 4 * B),
            (1, 3, left, 1, B, 3 * B),
            (2, 0, right, 0, 2 * B, 3 * B),
        )
    ]
    all_start(d_halo)

    for own in (0, 1):
        for row in range(3):
            where = (own, pl.ds(row * SUP, SUP), slice(None))
            acc[where] = near(zb, db.at[own + 1], own, row, (0, 1, 2))
            acc2[where] = near(db, db.at[own + 1], own, row, local[own])

    all_of(part_a, n_plane - 1, sum_recv.at[0]).wait()
    part_b[z_here] = jnp.sum(part_a[...], axis=0)
    for step in z_steps:
        sum_copy(part_b, z_here, 1, along_z(step)).start()

    all_arrived(d_halo)
    for own in (0, 1):
        for row in range(3):
            total = acc2[own, pl.ds(row * SUP, SUP), :]
            extra = near(db, db.at[own + 1], own, row, (halo[own],))
            if extra is not None:
                total = total + extra
            for r, c, column, offset in blocks_of(own, row):
                block = total[r * B : (r + 1) * B, c * B : (c + 1) * B]
                block = (block * present(column, offset)).astype(jnp.bfloat16)
                eb[own, pl.ds((2 * row + r) * B, B), pl.ds(c * B, B)] = block

    for own in (0, 1):
        for row in range(3):
            total = 0.375 * near(zb, eb.at[own], own, row, (0, 1, 2))
            total = total + 0.5 * acc[own, pl.ds(row * SUP, SUP), :]
            for r, c, column, offset in blocks_of(own, row):
                block = total[r * B : (r + 1) * B, c * B : (c + 1) * B]
                base = zb[own + 1, pl.ds((2 * row + r) * B, B), pl.ds(c * B, B)]
                block = (block + base.astype(jnp.float32)) * present(column, offset)
                out[column, offset] = block.astype(jnp.bfloat16)

    @pl.when(inner_right)
    def _():
        all_sent(s_raw_right + s_own_right + z_raw_right + t_right)

    @pl.when(jnp.logical_not(inner_right))
    def _():
        all_sent(z_raw_edge)

    all_sent(s_raw_left + s_own_left + z_raw_left + z_own_left + z_own_right + t_left + d_halo)
    all_of(part_a, n_plane - 1, sum_send.at[0]).wait()
    all_of(part_b, n_z - 1, sum_send.at[1]).wait()

    all_of(part_b, n_z - 1, sum_recv.at[1]).wait()
    total = jnp.sum(jnp.sum(part_b[...], axis=0), axis=1, keepdims=True)
    norm[...] = jnp.sqrt(total / (count * COLS * B))


def in_hbm(array):
    return pltpu.with_memory_space_constraint(array, pltpu.HBM)


def solution(mesh):
    n_grp, n_slab = mesh.shape["grp"], mesh.shape["slab"]
    n_plane, n_z = n_grp * PLANE, n_slab // PLANE

    def step(margin, factor, pattern):
        bands = pltpu.VMEM((4, BAND, SUP), jnp.bfloat16)
        pairs = pltpu.VMEM((2, BAND, SUP), jnp.bfloat16)
        wide = pltpu.VMEM((2, BAND, SUP), jnp.float32)
        corner = pltpu.VMEM((2, SUP, SUP), jnp.bfloat16)
        refined, norm = pl.pallas_call(
            functools.partial(kernel, n_grp, n_slab),
            out_shape=(
                jax.ShapeDtypeStruct((COLS, OFFS, B, B), jnp.bfloat16),
                jax.ShapeDtypeStruct((1, 1), jnp.float32),
            ),
            in_specs=[
                pl.BlockSpec(memory_space=pltpu.HBM),
                pl.BlockSpec(memory_space=pltpu.HBM),
                pl.BlockSpec(memory_space=pltpu.HBM),
            ],
            out_specs=(
                pl.BlockSpec(memory_space=pltpu.VMEM),
                pl.BlockSpec(memory_space=pltpu.VMEM),
            ),
            scratch_shapes=[
                bands,
                bands,
                bands,
                pairs,
                bands,
                pairs,
                corner,
                corner,
                corner,
                wide,
                wide,
                pltpu.VMEM((n_plane, 1, B), jnp.float32),
                pltpu.VMEM((n_z, 1, B), jnp.float32),
                pltpu.SemaphoreType.DMA((2 * COLS,)),
                pltpu.SemaphoreType.DMA((COPIES,)),
                pltpu.SemaphoreType.DMA((COPIES,)),
                pltpu.SemaphoreType.DMA((2,)),
                pltpu.SemaphoreType.DMA((2,)),
                pltpu.SemaphoreType.REGULAR((7,)),
                pltpu.SMEM((COLS, OFFS), jnp.int32),
                pltpu.SemaphoreType.DMA,
            ],
            compiler_params=pltpu.CompilerParams(
                collective_id=0, has_side_effects=True, vmem_limit_bytes=24 << 20
            ),
        )(
            in_hbm(margin.reshape(COLS, OFFS * B, B)),
            in_hbm(factor.reshape(COLS, OFFS * B, B)),
            in_hbm(pattern),
        )
        return refined, norm.reshape(())

    return jax.shard_map(
        step,
        mesh=mesh,
        in_specs=(
            P(("grp", "slab"), None, None, None),
            P(("grp", "slab"), None, None, None),
            P(("grp", "slab"), None),
        ),
        out_specs=(P(("grp", "slab"), None, None, None), P()),
        check_vma=False,
    )
```

```python
import functools

import jax
import jax.numpy as jnp
from jax import lax
from jax.experimental import pallas as pl
from jax.experimental.pallas import tpu as pltpu
from jax.sharding import PartitionSpec as P

B = 128
W = 2
OFFS = 2 * W + 1
COLS = 4
SUP = 2 * B
BAND = 3 * SUP
PLANE = 8
COPIES = 30
MESH = pl.DeviceIdType.MESH


def dot(left, right):
    return jnp.dot(left, right, preferred_element_type=jnp.float32)


def kernel(
    n_grp,
    n_slab,
    margin,
    factor,
    pattern,
    out,
    norm,
    sb,
    zb,
    zt,
    pb,
    db,
    eb,
    tu,
    td,
    ts,
    acc,
    acc2,
    part_a,
    part_b,
    load_sem,
    send_sem,
    recv_sem,
    sum_send,
    sum_recv,
    known,
    pat,
    pat_sem,
):
    grp = lax.axis_index("grp")
    slab = lax.axis_index("slab")
    count = n_grp * n_slab
    n_plane = n_grp * PLANE
    n_z = n_slab // PLANE
    here = grp * n_slab + slab

    def device(flat):
        return (lax.div(flat, n_slab), lax.rem(flat, n_slab))

    right = device(lax.rem(here + 1, count))
    left = device(lax.rem(here + count - 1, count))
    z_here = lax.div(slab, PLANE)
    in_plane = grp * PLANE + lax.rem(slab, PLANE)

    row_here, core = lax.div(lax.rem(slab, PLANE), 2), lax.rem(slab, 2)
    n_row = PLANE // 2

    def along_x(step):
        return (lax.rem(grp + n_grp + step, n_grp), slab)

    def along_y(step):
        return (grp, z_here * PLANE + lax.rem(row_here + n_row + step, n_row) * 2 + core)

    def along_z(step):
        return (grp, lax.rem(slab + n_slab + step * PLANE, n_slab))

    mate = (grp, slab + 1 - 2 * core)

    def signal(sem, *peers):
        for peer in peers:
            pl.semaphore_signal(sem, inc=1, device_id=peer, device_id_type=MESH)

    barrier = pltpu.get_barrier_semaphore()
    near_by = (left, right, along_y(1), along_y(-1), along_x(1), along_x(-1), along_z(1), along_z(-1))
    signal(barrier, *near_by)

    pattern_copy = pltpu.make_async_copy(pattern, pat, pat_sem)
    pattern_copy.start()
    loads = {}
    for which, (source, band) in enumerate(((margin, sb), (factor, zb))):
        for column in range(COLS):
            half = column % 2
            copy = pltpu.make_async_copy(
                source.at[column],
                band.at[1 + column // 2, pl.ds(half * B, OFFS * B), pl.ds(half * B, B)],
                load_sem.at[2 * column + which],
            )
            copy.start()
            loads[which, column] = copy

    blank = jnp.zeros((B, B), jnp.bfloat16)
    for band in (sb, zb, db):
        for index in range(4):
            band[index, pl.ds(5 * B, B), pl.ds(0, B)] = blank
            band[index, pl.ds(0, B), pl.ds(B, B)] = blank
    for index in range(2):
        eb[index, pl.ds(5 * B, B), pl.ds(0, B)] = blank
        eb[index, pl.ds(0, B), pl.ds(B, B)] = blank

    inner_left, inner_right = slab > 0, slab < n_slab - 1

    @pl.when(jnp.logical_not(inner_left))
    def _():
        sb[0, pl.ds(SUP, 2 * SUP), :] = jnp.zeros((2 * SUP, SUP), jnp.bfloat16)
        zb[0, pl.ds(2 * SUP, SUP), :] = jnp.zeros((SUP, SUP), jnp.bfloat16)
        tu[0] = jnp.zeros((SUP, SUP), jnp.bfloat16)

    @pl.when(jnp.logical_not(inner_right))
    def _():
        sb[3, pl.ds(0, 2 * SUP), :] = jnp.zeros((2 * SUP, SUP), jnp.bfloat16)
        zb[3, pl.ds(0, SUP), :] = jnp.zeros((SUP, SUP), jnp.bfloat16)
        td[1] = jnp.zeros((SUP, SUP), jnp.bfloat16)

    def present(column, offset):
        return pat[column, offset].astype(jnp.float32)

    first = inner_left.astype(jnp.float32)
    last = inner_right.astype(jnp.float32)

    def place(index, half, block, blocks=1):
        return (index, pl.ds(block * B, blocks * B), pl.ds(half * B, B))

    def scale_block(band, where, scale):
        factors = jnp.full((B, B), scale, jnp.float32).astype(jnp.bfloat16)
        band[where] = band[where] * factors

    pl.semaphore_wait(barrier, len(near_by))

    used = iter(range(COPIES))

    def remote(source, target, peer):
        index = next(used)
        return pltpu.make_async_remote_copy(
            src_ref=source,
            dst_ref=target,
            send_sem=send_sem.at[index],
            recv_sem=recv_sem.at[index],
            device_id=peer,
            device_id_type=MESH,
        )

    def all_start(copies):
        for copy in copies:
            copy.start()

    def all_arrived(copies):
        for copy in copies:
            copy.wait_recv()

    def all_sent(copies):
        for copy in copies:
            copy.wait_send()

    raw_left, raw_right = ((0, 0, 3), (1, 0, 1), (1, 2, 1)), ((3, 2, 3), (2, 2, 1), (2, 4, 1))
    edge_left, edge_right = ((0, 2, 1), (1, 2, 1)), ((2, 2, 1), (3, 2, 1))
    own_left, own_right = ((0, 3), (1, 1)), ((2, 3), (3, 1))

    def raw(source, band, pieces, target, peer):
        return [
            remote(
                source.at[column, pl.ds(offset * B, offsets * B), :],
                band.at[place(target, column % 2, offset + column % 2, offsets)],
                peer,
            )
            for column, offset, offsets in pieces
        ]

    def masked(band, pieces, target, peer):
        return [
            remote(
                band.at[place(1 + column // 2, column % 2, offset + column % 2)],
                band.at[place(target, column % 2, offset + column % 2)],
                peer,
            )
            for column, offset in pieces
        ]

    s_raw_left = raw(margin, sb, raw_left, 3, left)
    s_raw_right = raw(margin, sb, raw_right, 0, right)
    z_raw_left = raw(factor, zb, raw_left, 3, left)
    z_raw_right = raw(factor, zb, raw_right, 0, right)
    z_edge_left = raw(factor, zb, edge_left, 3, left)
    z_edge_right = raw(factor, zb, edge_right, 0, right)
    s_own_left, s_own_right = masked(sb, own_left, 3, left), masked(sb, own_right, 0, right)
    z_own_left, z_own_right = masked(zb, own_left, 3, left), masked(zb, own_right, 0, right)

    @pl.when(inner_right)
    def _():
        all_start(s_raw_right)

    @pl.when(inner_left)
    def _():
        all_start(s_raw_left)

    @pl.when(inner_right)
    def _():
        all_start(z_raw_right)

    @pl.when(jnp.logical_not(inner_right))
    def _():
        all_start(z_edge_right)

    @pl.when(inner_left)
    def _():
        all_start(z_raw_left)

    @pl.when(jnp.logical_not(inner_left))
    def _():
        all_start(z_edge_left)

    signal(known.at[0], along_y(1), along_y(-1))
    signal(known.at[3], along_z(1), along_z(-1))
    pattern_copy.wait()

    def mask_own(which, band):
        for column in range(COLS):
            loads[which, column].wait()
        for column in range(COLS):
            half = column % 2
            for offset in range(OFFS):
                if offset == W:
                    continue
                scale = present(column, offset)
                row = column + offset - W
                if which == 1 and row < 0:
                    scale = scale * first
                if which == 1 and row >= COLS:
                    scale = scale * last
                scale_block(band, place(1 + column // 2, half, half + offset), scale)

    mask_own(0, sb)

    @pl.when(inner_right)
    def _():
        all_start(s_own_right)

    @pl.when(inner_left)
    def _():
        all_start(s_own_left)

    mask_own(1, zb)
    all_start(z_own_right + z_own_left)

    def mask_low(band):
        for half, block, column, offset in ((0, 4, 0, 0), (1, 4, 0, 1), (1, 5, 1, 0)):
            scale_block(band, place(0, half, block), present(column, offset))

    def mask_high(band):
        for half, block, column, offset in ((0, 0, 2, 4), (0, 1, 3, 3), (1, 1, 3, 4)):
            scale_block(band, place(3, half, block), present(column, offset))

    pl.semaphore_wait(known.at[0], 2)
    signal(known.at[1], mate)
    pl.semaphore_wait(known.at[3], 2)
    signal(known.at[4], along_z(2), along_z(-2))

    def flip(inner, outer):
        value = zb[outer + 1, pl.ds((inner - outer + 1) * SUP, SUP), :]
        zt[inner + 1, pl.ds((outer - inner + 1) * SUP, SUP), :] = value.T

    for outer in (0, 1):
        for inner in (outer - 1, outer, outer + 1):
            flip(inner, outer)

    def upper(column):
        return dot(zt[column, pl.ds(2 * SUP, SUP), :], sb[column + 1, pl.ds(0, SUP), :])

    def lower(column):
        return dot(zt[column + 2, pl.ds(0, SUP), :], sb[column + 1, pl.ds(2 * SUP, SUP), :])

    ts[0] = lower(0).astype(jnp.bfloat16)
    ts[1] = upper(1).astype(jnp.bfloat16)
    t_left, t_right = [remote(ts.at[0], td.at[1], left)], [remote(ts.at[1], tu.at[0], right)]

    @pl.when(inner_right)
    def _():
        all_start(t_right)

    @pl.when(inner_left)
    def _():
        all_start(t_left)

    tu[1] = upper(0).astype(jnp.bfloat16)
    td[0] = lower(1).astype(jnp.bfloat16)

    def near(bands, values, own, row, inners):
        total = None
        for inner in inners:
            if abs(row - inner) > 1:
                continue
            term = dot(
                bands[own + inner, pl.ds((row - inner + 1) * SUP, SUP), :],
                values[pl.ds(inner * SUP, SUP), :],
            )
            total = term if total is None else total + term
        return total

    local = {0: (1, 2), 1: (0, 1)}
    halo = {0: 0, 1: 2}

    for own in (0, 1):
        for row in range(3):
            acc[own, pl.ds(row * SUP, SUP), :] = near(sb, zb.at[own + 1], own, row, local[own])

    pl.semaphore_wait(known.at[1], 1)
    signal(known.at[2], along_x(1), along_x(-1))
    pl.semaphore_wait(known.at[4], 2)
    signal(known.at[5], along_z(4), along_z(-4))

    @pl.when(inner_left)
    def _():
        all_arrived(s_raw_right + s_own_right)
        mask_low(sb)

    @pl.when(inner_right)
    def _():
        all_arrived(s_raw_left + s_own_left)
        mask_high(sb)

    for own in (0, 1):
        for row in range(3):
            where = (own, pl.ds(row * SUP, SUP), slice(None))
            total = acc[where]
            extra = near(sb, zb.at[own + 1], own, row, (halo[own],))
            if extra is not None:
                total = total + extra
            pb[where] = total.astype(jnp.bfloat16)

    eye = (
        lax.broadcasted_iota(jnp.int32, (B, B), 0) == lax.broadcasted_iota(jnp.int32, (B, B), 1)
    ).astype(jnp.float32)

    def blocks_of(own, row):
        for r in range(2):
            for c in range(2):
                offset = 2 * row + r - c
                if 0 <= offset < OFFS:
                    yield r, c, 2 * own + c, offset

    squares = jnp.zeros((8, B), jnp.float32)

    def defect(own, row, total, squares):
        for r, c, column, offset in blocks_of(own, row):
            block = -total[r * B : (r + 1) * B, c * B : (c + 1) * B]
            if offset == W:
                block = eye + block
            else:
                block = block * present(column, offset)
            block = block.astype(jnp.bfloat16)
            db[own + 1, pl.ds((2 * row + r) * B, B), pl.ds(c * B, B)] = block
            wide = block.astype(jnp.float32)
            squares = squares + jnp.sum((wide * wide).reshape(B // 8, 8, B), axis=0)
        return squares

    def outer(own, row):
        corner = (tu, td)[row // 2]
        return dot(corner[own], zb[own + 1, pl.ds(row * SUP, SUP), :])

    for own, rows in ((0, (1, 2)), (1, (0, 1))):
        for row in rows:
            total = near(zt, pb.at[own], own, row, (0, 1, 2))
            if row != 1:
                total = total + outer(own, row)
            squares = defect(own, row, total, squares)

    pl.semaphore_wait(known.at[2], 2)
    signal(known.at[6], along_x(2))
    pl.semaphore_wait(known.at[5], 2)

    @pl.when(inner_left)
    def _():
        all_arrived(z_raw_right)
        mask_low(zb)

    @pl.when(jnp.logical_not(inner_left))
    def _():
        all_arrived(z_edge_right)

    @pl.when(inner_right)
    def _():
        all_arrived(z_raw_left)
        mask_high(zb)

    @pl.when(jnp.logical_not(inner_right))
    def _():
        all_arrived(z_edge_left)

    all_arrived(z_own_right + z_own_left)
    flip(-1, -1)
    flip(0, -1)
    flip(1, 2)
    flip(2, 2)
    edges = ((0, 0), (1, 2))
    for own, row in edges:
        acc[own, pl.ds(row * SUP, SUP), :] = near(zt, pb.at[own], own, row, (0, 1, 2))
    @pl.when(inner_left)
    def _():
        all_arrived(t_right)

    @pl.when(inner_right)
    def _():
        all_arrived(t_left)

    for own, row in edges:
        total = acc[own, pl.ds(row * SUP, SUP), :] + outer(own, row)
        squares = defect(own, row, total, squares)

    part_a[in_plane] = jnp.sum(squares, axis=0, keepdims=True)
    pl.semaphore_wait(known.at[6], 1)

    def sum_copy(buffer, slot, stage, peer):
        return pltpu.make_async_remote_copy(
            src_ref=buffer.at[slot],
            dst_ref=buffer.at[slot],
            send_sem=sum_send.at[stage],
            recv_sem=sum_recv.at[stage],
            device_id=peer,
            device_id_type=MESH,
        )

    def hops(step, size):
        return min(step, size - step)

    plane_steps = sorted(
        ((x, y, c) for x in range(n_grp) for y in range(n_row) for c in range(2) if x or y or c),
        key=lambda step: -hops(step[0], n_grp) - hops(step[1], n_row),
    )
    z_steps = sorted(range(1, n_z), key=lambda step: -hops(step, n_z))

    def all_of(buffer, rows, sem):
        return pltpu.make_async_copy(buffer.at[pl.ds(0, rows)], buffer.at[pl.ds(0, rows)], sem)

    x_of = [lax.rem(grp + step, n_grp) for step in range(n_grp)]
    y_of = [z_here * PLANE + 2 * lax.rem(row_here + step, n_row) for step in range(n_row)]
    core_of = (core, 1 - core)
    for x, y, c in plane_steps:
        sum_copy(part_a, in_plane, 0, (x_of[x], y_of[y] + core_of[c])).start()
    d_halo = [
        remote(
            db.at[index, pl.ds(first_row, rows), pl.ds(half * B, B)],
            db.at[target, pl.ds(first_row, rows), pl.ds(half * B, B)],
            peer,
        )
        for index, target, peer, half, first_row, rows in (
            (1, 3, left, 0, 0, 4 * B),
            (2, 0, right, 1, 2 * B, 4 * B),
            (1, 3, left, 1, B, 3 * B),
            (2, 0, right, 0, 2 * B, 3 * B),
        )
    ]
    all_start(d_halo)

    for own in (0, 1):
        for row in range(3):
            where = (own, pl.ds(row * SUP, SUP), slice(None))
            acc[where] = near(zb, db.at[own + 1], own, row, (0, 1, 2))
            acc2[where] = near(db, db.at[own + 1], own, row, local[own])

    all_of(part_a, n_plane - 1, sum_recv.at[0]).wait()
    part_b[z_here] = jnp.sum(part_a[...], axis=0)
    for step in z_steps:
        sum_copy(part_b, z_here, 1, along_z(step)).start()

    all_arrived(d_halo)
    for own in (0, 1):
        for row in range(3):
            total = acc2[own, pl.ds(row * SUP, SUP), :]
            extra = near(db, db.at[own + 1], own, row, (halo[own],))
            if extra is not None:
                total = total + extra
            for r, c, column, offset in blocks_of(own, row):
                block = total[r * B : (r + 1) * B, c * B : (c + 1) * B]
                block = (block * present(column, offset)).astype(jnp.bfloat16)
                eb[own, pl.ds((2 * row + r) * B, B), pl.ds(c * B, B)] = block

    for own in (0, 1):
        for row in range(3):
            total = 0.375 * near(zb, eb.at[own], own, row, (0, 1, 2))
            total = total + 0.5 * acc[own, pl.ds(row * SUP, SUP), :]
            for r, c, column, offset in blocks_of(own, row):
                block = total[r * B : (r + 1) * B, c * B : (c + 1) * B]
                base = zb[own + 1, pl.ds((2 * row + r) * B, B), pl.ds(c * B, B)]
                block = (block + base.astype(jnp.float32)) * present(column, offset)
                out[column, offset] = block.astype(jnp.bfloat16)

    @pl.when(inner_right)
    def _():
        all_sent(s_raw_right + s_own_right + z_raw_right + t_right)

    @pl.when(jnp.logical_not(inner_right))
    def _():
        all_sent(z_edge_right)

    @pl.when(inner_left)
    def _():
        all_sent(s_raw_left + s_own_left + z_raw_left + t_left)

    @pl.when(jnp.logical_not(inner_left))
    def _():
        all_sent(z_edge_left)

    all_sent(z_own_left + z_own_right + d_halo)
    all_of(part_a, n_plane - 1, sum_send.at[0]).wait()
    all_of(part_b, n_z - 1, sum_send.at[1]).wait()

    all_of(part_b, n_z - 1, sum_recv.at[1]).wait()
    total = jnp.sum(jnp.sum(part_b[...], axis=0), axis=1, keepdims=True)
    norm[...] = jnp.broadcast_to(jnp.sqrt(total / (count * COLS * B)), (8, B))


def in_hbm(array):
    return pltpu.with_memory_space_constraint(array, pltpu.HBM)


def solution(mesh):
    n_grp, n_slab = mesh.shape["grp"], mesh.shape["slab"]
    n_plane, n_z = n_grp * PLANE, n_slab // PLANE

    def step(margin, factor, pattern):
        bands = pltpu.VMEM((4, BAND, SUP), jnp.bfloat16)
        pairs = pltpu.VMEM((2, BAND, SUP), jnp.bfloat16)
        wide = pltpu.VMEM((2, BAND, SUP), jnp.float32)
        corner = pltpu.VMEM((2, SUP, SUP), jnp.bfloat16)
        refined, norm = pl.pallas_call(
            functools.partial(kernel, n_grp, n_slab),
            out_shape=(
                jax.ShapeDtypeStruct((COLS, OFFS, B, B), jnp.bfloat16),
                jax.ShapeDtypeStruct((8, B), jnp.float32),
            ),
            in_specs=[
                pl.BlockSpec(memory_space=pltpu.HBM),
                pl.BlockSpec(memory_space=pltpu.HBM),
                pl.BlockSpec(memory_space=pltpu.HBM),
            ],
            out_specs=(
                pl.BlockSpec(memory_space=pltpu.VMEM),
                pl.BlockSpec(memory_space=pltpu.VMEM),
            ),
            scratch_shapes=[
                bands,
                bands,
                bands,
                pairs,
                bands,
                pairs,
                corner,
                corner,
                corner,
                wide,
                wide,
                pltpu.VMEM((n_plane, 1, B), jnp.float32),
                pltpu.VMEM((n_z, 1, B), jnp.float32),
                pltpu.SemaphoreType.DMA((2 * COLS,)),
                pltpu.SemaphoreType.DMA((COPIES,)),
                pltpu.SemaphoreType.DMA((COPIES,)),
                pltpu.SemaphoreType.DMA((2,)),
                pltpu.SemaphoreType.DMA((2,)),
                pltpu.SemaphoreType.REGULAR((7,)),
                pltpu.SMEM((COLS, OFFS), jnp.int32),
                pltpu.SemaphoreType.DMA,
            ],
            compiler_params=pltpu.CompilerParams(
                collective_id=0, has_side_effects=True, vmem_limit_bytes=24 << 20
            ),
        )(
            in_hbm(margin.reshape(COLS, OFFS * B, B)),
            in_hbm(factor.reshape(COLS, OFFS * B, B)),
            in_hbm(pattern),
        )
        return refined, norm[0, 0]

    return jax.shard_map(
        step,
        mesh=mesh,
        in_specs=(
            P(("grp", "slab"), None, None, None),
            P(("grp", "slab"), None, None, None),
            P(("grp", "slab"), None),
        ),
        out_specs=(P(("grp", "slab"), None, None, None), P()),
        check_vma=False,
    )
```

```python
import functools

import jax
import jax.numpy as jnp
from jax import lax
from jax.experimental import pallas as pl
from jax.experimental.pallas import tpu as pltpu
from jax.sharding import PartitionSpec as P

B = 128
W = 2
OFFS = 2 * W + 1
COLS = 4
SUP = 2 * B
BAND = 3 * SUP
PLANE = 8
COPIES = 30
MESH = pl.DeviceIdType.MESH


def dot(left, right):
    return jnp.dot(left, right, preferred_element_type=jnp.float32)


def kernel(
    n_grp,
    n_slab,
    margin,
    factor,
    pattern,
    out,
    norm,
    sb,
    zb,
    zt,
    pb,
    db,
    eb,
    tu,
    td,
    ts,
    acc,
    acc2,
    part_a,
    part_b,
    load_sem,
    send_sem,
    recv_sem,
    sum_send,
    sum_recv,
    known,
    pat,
    pat_sem,
):
    grp = lax.axis_index("grp")
    slab = lax.axis_index("slab")
    count = n_grp * n_slab
    n_plane = n_grp * PLANE
    n_z = n_slab // PLANE
    here = grp * n_slab + slab

    def device(flat):
        return (lax.div(flat, n_slab), lax.rem(flat, n_slab))

    right = device(lax.rem(here + 1, count))
    left = device(lax.rem(here + count - 1, count))
    z_here = lax.div(slab, PLANE)
    in_plane = grp * PLANE + lax.rem(slab, PLANE)

    row_here, core = lax.div(lax.rem(slab, PLANE), 2), lax.rem(slab, 2)
    n_row = PLANE // 2

    def along_x(step):
        return (lax.rem(grp + n_grp + step, n_grp), slab)

    def along_y(step):
        return (grp, z_here * PLANE + lax.rem(row_here + n_row + step, n_row) * 2 + core)

    def along_z(step):
        return (grp, lax.rem(slab + n_slab + step * PLANE, n_slab))

    mate = (grp, slab + 1 - 2 * core)

    def signal(sem, *peers):
        for peer in peers:
            pl.semaphore_signal(sem, inc=1, device_id=peer, device_id_type=MESH)

    barrier = pltpu.get_barrier_semaphore()
    near_by = (left, right, along_y(1), along_y(-1), along_x(1), along_x(-1), along_z(1), along_z(-1))
    signal(barrier, *near_by)

    pattern_copy = pltpu.make_async_copy(pattern, pat, pat_sem)
    pattern_copy.start()
    loads = {}
    for which, (source, band) in enumerate(((margin, sb), (factor, zb))):
        for column in range(COLS):
            half = column % 2
            copy = pltpu.make_async_copy(
                source.at[column],
                band.at[1 + column // 2, pl.ds(half * B, OFFS * B), pl.ds(half * B, B)],
                load_sem.at[2 * column + which],
            )
            copy.start()
            loads[which, column] = copy

    blank = jnp.zeros((B, B), jnp.bfloat16)
    for band in (sb, zb, db):
        for index in range(4):
            band[index, pl.ds(5 * B, B), pl.ds(0, B)] = blank
            band[index, pl.ds(0, B), pl.ds(B, B)] = blank
    for index in range(2):
        eb[index, pl.ds(5 * B, B), pl.ds(0, B)] = blank
        eb[index, pl.ds(0, B), pl.ds(B, B)] = blank

    inner_left, inner_right = slab > 0, slab < n_slab - 1

    @pl.when(jnp.logical_not(inner_left))
    def _():
        sb[0, pl.ds(SUP, 2 * SUP), :] = jnp.zeros((2 * SUP, SUP), jnp.bfloat16)
        zb[0, pl.ds(2 * SUP, SUP), :] = jnp.zeros((SUP, SUP), jnp.bfloat16)
        tu[0] = jnp.zeros((SUP, SUP), jnp.bfloat16)

    @pl.when(jnp.logical_not(inner_right))
    def _():
        sb[3, pl.ds(0, 2 * SUP), :] = jnp.zeros((2 * SUP, SUP), jnp.bfloat16)
        zb[3, pl.ds(0, SUP), :] = jnp.zeros((SUP, SUP), jnp.bfloat16)
        td[1] = jnp.zeros((SUP, SUP), jnp.bfloat16)

    def present(column, offset):
        return pat[column, offset].astype(jnp.float32)

    first = inner_left.astype(jnp.float32)
    last = inner_right.astype(jnp.float32)

    def place(index, half, block, blocks=1):
        return (index, pl.ds(block * B, blocks * B), pl.ds(half * B, B))

    def scale_block(band, where, scale):
        factors = jnp.full((B, B), scale, jnp.float32).astype(jnp.bfloat16)
        band[where] = band[where] * factors

    pl.semaphore_wait(barrier, len(near_by))

    used = iter(range(COPIES))

    def remote(source, target, peer):
        index = next(used)
        return pltpu.make_async_remote_copy(
            src_ref=source,
            dst_ref=target,
            send_sem=send_sem.at[index],
            recv_sem=recv_sem.at[index],
            device_id=peer,
            device_id_type=MESH,
        )

    def all_start(copies):
        for copy in copies:
            copy.start()

    def all_arrived(copies):
        for copy in copies:
            copy.wait_recv()

    def all_sent(copies):
        for copy in copies:
            copy.wait_send()

    raw_left, raw_right = ((0, 0, 3), (1, 0, 1), (1, 2, 1)), ((3, 2, 3), (2, 2, 1), (2, 4, 1))
    edge_left, edge_right = ((0, 2, 1), (1, 2, 1)), ((2, 2, 1), (3, 2, 1))
    own_left, own_right = ((0, 3), (1, 1)), ((2, 3), (3, 1))

    def raw(source, band, pieces, target, peer):
        return [
            remote(
                source.at[column, pl.ds(offset * B, offsets * B), :],
                band.at[place(target, column % 2, offset + column % 2, offsets)],
                peer,
            )
            for column, offset, offsets in pieces
        ]

    def masked(band, pieces, target, peer):
        return [
            remote(
                band.at[place(1 + column // 2, column % 2, offset + column % 2)],
                band.at[place(target, column % 2, offset + column % 2)],
                peer,
            )
            for column, offset in pieces
        ]

    s_raw_left = raw(margin, sb, raw_left, 3, left)
    s_raw_right = raw(margin, sb, raw_right, 0, right)
    z_raw_left = raw(factor, zb, raw_left, 3, left)
    z_raw_right = raw(factor, zb, raw_right, 0, right)
    z_edge_left = raw(factor, zb, edge_left, 3, left)
    z_edge_right = raw(factor, zb, edge_right, 0, right)
    s_own_left, s_own_right = masked(sb, own_left, 3, left), masked(sb, own_right, 0, right)
    z_own_left, z_own_right = masked(zb, own_left, 3, left), masked(zb, own_right, 0, right)

    @pl.when(inner_left)
    def _():
        all_start(s_raw_left)

    @pl.when(inner_right)
    def _():
        all_start(s_raw_right)

    @pl.when(inner_left)
    def _():
        all_start(z_raw_left)

    @pl.when(jnp.logical_not(inner_left))
    def _():
        all_start(z_edge_left)

    @pl.when(inner_right)
    def _():
        all_start(z_raw_right)

    @pl.when(jnp.logical_not(inner_right))
    def _():
        all_start(z_edge_right)

    signal(known.at[0], along_y(1), along_y(-1))
    signal(known.at[3], along_z(1), along_z(-1))
    pattern_copy.wait()

    def mask_own(which, band):
        for column in range(COLS):
            loads[which, column].wait()
        for column in range(COLS):
            half = column % 2
            for offset in range(OFFS):
                if offset == W:
                    continue
                scale = present(column, offset)
                row = column + offset - W
                if which == 1 and row < 0:
                    scale = scale * first
                if which == 1 and row >= COLS:
                    scale = scale * last
                scale_block(band, place(1 + column // 2, half, half + offset), scale)

    mask_own(0, sb)

    @pl.when(inner_left)
    def _():
        all_start(s_own_left)

    @pl.when(inner_right)
    def _():
        all_start(s_own_right)

    mask_own(1, zb)
    all_start(z_own_left + z_own_right)

    def mask_low(band):
        for half, block, column, offset in ((0, 4, 0, 0), (1, 4, 0, 1), (1, 5, 1, 0)):
            scale_block(band, place(0, half, block), present(column, offset))

    def mask_high(band):
        for half, block, column, offset in ((0, 0, 2, 4), (0, 1, 3, 3), (1, 1, 3, 4)):
            scale_block(band, place(3, half, block), present(column, offset))

    pl.semaphore_wait(known.at[0], 2)
    signal(known.at[1], mate)
    pl.semaphore_wait(known.at[3], 2)
    signal(known.at[4], along_z(2), along_z(-2))

    def flip(inner, outer):
        value = zb[outer + 1, pl.ds((inner - outer + 1) * SUP, SUP), :]
        zt[inner + 1, pl.ds((outer - inner + 1) * SUP, SUP), :] = value.T

    for outer in (0, 1):
        for inner in (outer - 1, outer, outer + 1):
            flip(inner, outer)

    def upper(column):
        return dot(zt[column, pl.ds(2 * SUP, SUP), :], sb[column + 1, pl.ds(0, SUP), :])

    def lower(column):
        return dot(zt[column + 2, pl.ds(0, SUP), :], sb[column + 1, pl.ds(2 * SUP, SUP), :])

    t_left, t_right = [remote(ts.at[0], td.at[1], left)], [remote(ts.at[1], tu.at[0], right)]
    ts[0] = lower(0).astype(jnp.bfloat16)

    @pl.when(inner_left)
    def _():
        all_start(t_left)

    ts[1] = upper(1).astype(jnp.bfloat16)

    @pl.when(inner_right)
    def _():
        all_start(t_right)

    tu[1] = upper(0).astype(jnp.bfloat16)
    td[0] = lower(1).astype(jnp.bfloat16)

    def near(bands, values, own, row, inners):
        total = None
        for inner in inners:
            if abs(row - inner) > 1:
                continue
            term = dot(
                bands[own + inner, pl.ds((row - inner + 1) * SUP, SUP), :],
                values[pl.ds(inner * SUP, SUP), :],
            )
            total = term if total is None else total + term
        return total

    local = {0: (1, 2), 1: (0, 1)}
    halo = {0: 0, 1: 2}

    for own in (0, 1):
        for row in range(3):
            acc[own, pl.ds(row * SUP, SUP), :] = near(sb, zb.at[own + 1], own, row, local[own])

    pl.semaphore_wait(known.at[1], 1)
    signal(known.at[2], along_x(1), along_x(-1))
    pl.semaphore_wait(known.at[4], 2)
    signal(known.at[5], along_z(4), along_z(-4))

    @pl.when(inner_left)
    def _():
        all_arrived(s_raw_right + s_own_right)
        mask_low(sb)

    @pl.when(inner_right)
    def _():
        all_arrived(s_raw_left + s_own_left)
        mask_high(sb)

    for own in (0, 1):
        for row in range(3):
            where = (own, pl.ds(row * SUP, SUP), slice(None))
            total = acc[where]
            extra = near(sb, zb.at[own + 1], own, row, (halo[own],))
            if extra is not None:
                total = total + extra
            pb[where] = total.astype(jnp.bfloat16)

    eye = (
        lax.broadcasted_iota(jnp.int32, (B, B), 0) == lax.broadcasted_iota(jnp.int32, (B, B), 1)
    ).astype(jnp.float32)

    def blocks_of(own, row):
        for r in range(2):
            for c in range(2):
                offset = 2 * row + r - c
                if 0 <= offset < OFFS:
                    yield r, c, 2 * own + c, offset

    squares = jnp.zeros((8, B), jnp.float32)

    def defect(own, row, total, squares):
        for r, c, column, offset in blocks_of(own, row):
            block = -total[r * B : (r + 1) * B, c * B : (c + 1) * B]
            if offset == W:
                block = eye + block
            else:
                block = block * present(column, offset)
            block = block.astype(jnp.bfloat16)
            db[own + 1, pl.ds((2 * row + r) * B, B), pl.ds(c * B, B)] = block
            wide = block.astype(jnp.float32)
            squares = squares + jnp.sum((wide * wide).reshape(B // 8, 8, B), axis=0)
        return squares

    def outer(own, row):
        corner = (tu, td)[row // 2]
        return dot(corner[own], zb[own + 1, pl.ds(row * SUP, SUP), :])

    for own, rows in ((0, (1, 2)), (1, (0, 1))):
        for row in rows:
            total = near(zt, pb.at[own], own, row, (0, 1, 2))
            if row != 1:
                total = total + outer(own, row)
            squares = defect(own, row, total, squares)

    pl.semaphore_wait(known.at[2], 2)
    signal(known.at[6], along_x(2))
    pl.semaphore_wait(known.at[5], 2)

    @pl.when(inner_left)
    def _():
        all_arrived(z_raw_right)
        mask_low(zb)

    @pl.when(jnp.logical_not(inner_left))
    def _():
        all_arrived(z_edge_right)

    @pl.when(inner_right)
    def _():
        all_arrived(z_raw_left)
        mask_high(zb)

    @pl.when(jnp.logical_not(inner_right))
    def _():
        all_arrived(z_edge_left)

    all_arrived(z_own_right + z_own_left)
    flip(-1, -1)
    flip(0, -1)
    flip(1, 2)
    flip(2, 2)
    edges = ((0, 0), (1, 2))
    for own, row in edges:
        acc[own, pl.ds(row * SUP, SUP), :] = near(zt, pb.at[own], own, row, (0, 1, 2))
    @pl.when(inner_left)
    def _():
        all_arrived(t_right)

    @pl.when(inner_right)
    def _():
        all_arrived(t_left)

    for own, row in edges:
        total = acc[own, pl.ds(row * SUP, SUP), :] + outer(own, row)
        squares = defect(own, row, total, squares)

    part_a[in_plane] = jnp.sum(squares, axis=0, keepdims=True)
    pl.semaphore_wait(known.at[6], 1)

    def sum_copy(buffer, slot, stage, peer):
        return pltpu.make_async_remote_copy(
            src_ref=buffer.at[slot],
            dst_ref=buffer.at[slot],
            send_sem=sum_send.at[stage],
            recv_sem=sum_recv.at[stage],
            device_id=peer,
            device_id_type=MESH,
        )

    def hops(step, size):
        return min(step, size - step)

    plane_steps = sorted(
        ((x, y, c) for x in range(n_grp) for y in range(n_row) for c in range(2) if x or y or c),
        key=lambda step: -hops(step[0], n_grp) - hops(step[1], n_row),
    )
    z_steps = sorted(range(1, n_z), key=lambda step: -hops(step, n_z))

    def all_of(buffer, rows, sem):
        return pltpu.make_async_copy(buffer.at[pl.ds(0, rows)], buffer.at[pl.ds(0, rows)], sem)

    x_of = [lax.rem(grp + step, n_grp) for step in range(n_grp)]
    y_of = [z_here * PLANE + 2 * lax.rem(row_here + step, n_row) for step in range(n_row)]
    core_of = (core, 1 - core)
    for x, y, c in plane_steps:
        sum_copy(part_a, in_plane, 0, (x_of[x], y_of[y] + core_of[c])).start()
    d_halo = [
        remote(
            db.at[index, pl.ds(first_row, rows), pl.ds(half * B, B)],
            db.at[target, pl.ds(first_row, rows), pl.ds(half * B, B)],
            peer,
        )
        for index, target, peer, half, first_row, rows in (
            (1, 3, left, 0, 0, 4 * B),
            (2, 0, right, 1, 2 * B, 4 * B),
            (1, 3, left, 1, B, 3 * B),
            (2, 0, right, 0, 2 * B, 3 * B),
        )
    ]
    all_start(d_halo)

    for own in (0, 1):
        for row in range(3):
            where = (own, pl.ds(row * SUP, SUP), slice(None))
            acc[where] = near(zb, db.at[own + 1], own, row, (0, 1, 2))
            acc2[where] = near(db, db.at[own + 1], own, row, local[own])

    all_of(part_a, n_plane - 1, sum_recv.at[0]).wait()
    part_b[z_here] = jnp.sum(part_a[...], axis=0)
    for step in z_steps:
        sum_copy(part_b, z_here, 1, along_z(step)).start()

    all_arrived(d_halo)
    for own in (0, 1):
        for row in range(3):
            total = acc2[own, pl.ds(row * SUP, SUP), :]
            extra = near(db, db.at[own + 1], own, row, (halo[own],))
            if extra is not None:
                total = total + extra
            for r, c, column, offset in blocks_of(own, row):
                block = total[r * B : (r + 1) * B, c * B : (c + 1) * B]
                block = (block * present(column, offset)).astype(jnp.bfloat16)
                eb[own, pl.ds((2 * row + r) * B, B), pl.ds(c * B, B)] = block

    for own in (0, 1):
        for row in range(3):
            total = 0.375 * near(zb, eb.at[own], own, row, (0, 1, 2))
            total = total + 0.5 * acc[own, pl.ds(row * SUP, SUP), :]
            for r, c, column, offset in blocks_of(own, row):
                block = total[r * B : (r + 1) * B, c * B : (c + 1) * B]
                base = zb[own + 1, pl.ds((2 * row + r) * B, B), pl.ds(c * B, B)]
                block = (block + base.astype(jnp.float32)) * present(column, offset)
                out[column, offset] = block.astype(jnp.bfloat16)

    @pl.when(inner_right)
    def _():
        all_sent(s_raw_right + s_own_right + z_raw_right + t_right)

    @pl.when(jnp.logical_not(inner_right))
    def _():
        all_sent(z_edge_right)

    @pl.when(inner_left)
    def _():
        all_sent(s_raw_left + s_own_left + z_raw_left + t_left)

    @pl.when(jnp.logical_not(inner_left))
    def _():
        all_sent(z_edge_left)

    all_sent(z_own_left + z_own_right + d_halo)
    all_of(part_a, n_plane - 1, sum_send.at[0]).wait()
    all_of(part_b, n_z - 1, sum_send.at[1]).wait()

    all_of(part_b, n_z - 1, sum_recv.at[1]).wait()
    total = jnp.sum(jnp.sum(part_b[...], axis=0), axis=1, keepdims=True)
    norm[...] = jnp.broadcast_to(jnp.sqrt(total / (count * COLS * B)), (8, B))


def finish(refined, norm, refined_out, norm_out, cell, sem):
    cell[...] = norm[0:1, 0:1]
    copies = [pltpu.make_async_copy(cell, norm_out, sem.at[COLS])]
    for column in range(COLS):
        copies.append(
            pltpu.make_async_copy(refined.at[column], refined_out.at[column], sem.at[column])
        )
    for copy in copies:
        copy.start()
    for copy in copies:
        copy.wait()


def in_hbm(array):
    return pltpu.with_memory_space_constraint(array, pltpu.HBM)


def solution(mesh):
    n_grp, n_slab = mesh.shape["grp"], mesh.shape["slab"]
    n_plane, n_z = n_grp * PLANE, n_slab // PLANE

    def step(margin, factor, pattern):
        bands = pltpu.VMEM((4, BAND, SUP), jnp.bfloat16)
        pairs = pltpu.VMEM((2, BAND, SUP), jnp.bfloat16)
        wide = pltpu.VMEM((2, BAND, SUP), jnp.float32)
        corner = pltpu.VMEM((2, SUP, SUP), jnp.bfloat16)
        refined, norm = pl.pallas_call(
            functools.partial(kernel, n_grp, n_slab),
            out_shape=(
                jax.ShapeDtypeStruct((COLS, OFFS, B, B), jnp.bfloat16),
                jax.ShapeDtypeStruct((8, B), jnp.float32),
            ),
            in_specs=[
                pl.BlockSpec(memory_space=pltpu.HBM),
                pl.BlockSpec(memory_space=pltpu.HBM),
                pl.BlockSpec(memory_space=pltpu.HBM),
            ],
            out_specs=(
                pl.BlockSpec(memory_space=pltpu.VMEM),
                pl.BlockSpec(memory_space=pltpu.VMEM),
            ),
            scratch_shapes=[
                bands,
                bands,
                bands,
                pairs,
                bands,
                pairs,
                corner,
                corner,
                corner,
                wide,
                wide,
                pltpu.VMEM((n_plane, 1, B), jnp.float32),
                pltpu.VMEM((n_z, 1, B), jnp.float32),
                pltpu.SemaphoreType.DMA((2 * COLS,)),
                pltpu.SemaphoreType.DMA((COPIES,)),
                pltpu.SemaphoreType.DMA((COPIES,)),
                pltpu.SemaphoreType.DMA((2,)),
                pltpu.SemaphoreType.DMA((2,)),
                pltpu.SemaphoreType.REGULAR((7,)),
                pltpu.SMEM((COLS, OFFS), jnp.int32),
                pltpu.SemaphoreType.DMA,
            ],
            compiler_params=pltpu.CompilerParams(
                collective_id=0, has_side_effects=True, vmem_limit_bytes=24 << 20
            ),
        )(
            in_hbm(margin.reshape(COLS, OFFS * B, B)),
            in_hbm(factor.reshape(COLS, OFFS * B, B)),
            in_hbm(pattern),
        )
        refined, norm = pl.pallas_call(
            finish,
            out_shape=(
                jax.ShapeDtypeStruct((COLS, OFFS, B, B), jnp.bfloat16),
                jax.ShapeDtypeStruct((1, 1), jnp.float32),
            ),
            in_specs=[pl.BlockSpec(memory_space=pltpu.VMEM)] * 2,
            out_specs=(pl.BlockSpec(memory_space=pl.ANY), pl.BlockSpec(memory_space=pl.ANY)),
            scratch_shapes=[
                pltpu.VMEM((1, 1), jnp.float32),
                pltpu.SemaphoreType.DMA((COLS + 1,)),
            ],
            compiler_params=pltpu.CompilerParams(vmem_limit_bytes=8 << 20),
        )(refined, norm)
        return refined, norm.reshape(())

    return jax.shard_map(
        step,
        mesh=mesh,
        in_specs=(
            P(("grp", "slab"), None, None, None),
            P(("grp", "slab"), None, None, None),
            P(("grp", "slab"), None),
        ),
        out_specs=(P(("grp", "slab"), None, None, None), P()),
        check_vma=False,
    )
```

```python
import functools

import jax
import jax.numpy as jnp
from jax import lax
from jax.experimental import pallas as pl
from jax.experimental.pallas import tpu as pltpu
from jax.sharding import PartitionSpec as P

B = 128
W = 2
OFFS = 2 * W + 1
COLS = 4
SUP = 2 * B
BAND = 3 * SUP
PLANE = 8
COPIES = 18
MESH = pl.DeviceIdType.MESH


def dot(left, right):
    return jnp.dot(left, right, preferred_element_type=jnp.float32)


def kernel(
    n_grp,
    n_slab,
    margin,
    factor,
    pattern,
    out,
    norm,
    sb,
    zb,
    zt,
    pb,
    db,
    eb,
    tu,
    td,
    ts,
    acc,
    acc2,
    part_a,
    part_b,
    load_sem,
    send_sem,
    recv_sem,
    sum_send,
    sum_recv,
    known,
    pat,
    pat_sem,
):
    grp = lax.axis_index("grp")
    slab = lax.axis_index("slab")
    count = n_grp * n_slab
    n_plane = n_grp * PLANE
    n_z = n_slab // PLANE
    here = grp * n_slab + slab

    def device(flat):
        return (lax.div(flat, n_slab), lax.rem(flat, n_slab))

    right = device(lax.rem(here + 1, count))
    left = device(lax.rem(here + count - 1, count))
    z_here = lax.div(slab, PLANE)
    in_plane = grp * PLANE + lax.rem(slab, PLANE)

    row_here, core = lax.div(lax.rem(slab, PLANE), 2), lax.rem(slab, 2)
    n_row = PLANE // 2

    def along_x(step):
        return (lax.rem(grp + n_grp + step, n_grp), slab)

    def along_y(step):
        return (grp, z_here * PLANE + lax.rem(row_here + n_row + step, n_row) * 2 + core)

    def along_z(step):
        return (grp, lax.rem(slab + n_slab + step * PLANE, n_slab))

    mate = (grp, slab + 1 - 2 * core)

    def signal(sem, *peers):
        for peer in peers:
            pl.semaphore_signal(sem, inc=1, device_id=peer, device_id_type=MESH)

    barrier = pltpu.get_barrier_semaphore()
    near_by = (left, right, along_y(1), along_y(-1), along_x(1), along_x(-1), along_z(1), along_z(-1))
    signal(barrier, *near_by)

    pattern_copy = pltpu.make_async_copy(pattern, pat, pat_sem)
    pattern_copy.start()
    loads = {}
    for which, (source, band) in enumerate(((margin, sb), (factor, zb))):
        for column in range(COLS):
            half = column % 2
            copy = pltpu.make_async_copy(
                source.at[column],
                band.at[1 + column // 2, pl.ds(half * B, OFFS * B), pl.ds(half * B, B)],
                load_sem.at[2 * column + which],
            )
            copy.start()
            loads[which, column] = copy

    blank = jnp.zeros((B, B), jnp.bfloat16)
    for band in (sb, zb, db):
        for index in range(4):
            band[index, pl.ds(5 * B, B), pl.ds(0, B)] = blank
            band[index, pl.ds(0, B), pl.ds(B, B)] = blank
    for index in range(2):
        eb[index, pl.ds(5 * B, B), pl.ds(0, B)] = blank
        eb[index, pl.ds(0, B), pl.ds(B, B)] = blank

    inner_left, inner_right = slab > 0, slab < n_slab - 1

    @pl.when(jnp.logical_not(inner_left))
    def _():
        sb[0, pl.ds(SUP, 2 * SUP), :] = jnp.zeros((2 * SUP, SUP), jnp.bfloat16)
        zb[0, pl.ds(2 * SUP, SUP), :] = jnp.zeros((SUP, SUP), jnp.bfloat16)
        tu[0] = jnp.zeros((SUP, SUP), jnp.bfloat16)

    @pl.when(jnp.logical_not(inner_right))
    def _():
        sb[3, pl.ds(0, 2 * SUP), :] = jnp.zeros((2 * SUP, SUP), jnp.bfloat16)
        zb[3, pl.ds(0, SUP), :] = jnp.zeros((SUP, SUP), jnp.bfloat16)
        td[1] = jnp.zeros((SUP, SUP), jnp.bfloat16)

    def present(column, offset):
        return pat[column, offset].astype(jnp.float32)

    first = inner_left.astype(jnp.float32)
    last = inner_right.astype(jnp.float32)

    def place(index, half, block, blocks=1):
        return (index, pl.ds(block * B, blocks * B), pl.ds(half * B, B))

    def scale_block(band, where, scale):
        factors = jnp.full((B, B), scale, jnp.float32).astype(jnp.bfloat16)
        band[where] = band[where] * factors

    used = iter(range(COPIES))

    def remote(source, target, peer):
        index = next(used)
        return pltpu.make_async_remote_copy(
            src_ref=source,
            dst_ref=target,
            send_sem=send_sem.at[index],
            recv_sem=recv_sem.at[index],
            device_id=peer,
            device_id_type=MESH,
        )

    def all_start(copies):
        for copy in copies:
            copy.start()

    def all_arrived(copies):
        for copy in copies:
            copy.wait_recv()

    def all_sent(copies):
        for copy in copies:
            copy.wait_send()

    pieces_left, pieces_right = ((0, 0, 4), (1, 0, 3)), ((2, 2, 3), (3, 1, 4))
    edge_left, edge_right = ((0, 2, 2), (1, 1, 2)), ((2, 2, 2), (3, 1, 2))

    def halo_copies(band, pieces, target, peer):
        return [
            remote(
                band.at[place(1 + column // 2, column % 2, offset + column % 2, offsets)],
                band.at[place(target, column % 2, offset + column % 2, offsets)],
                peer,
            )
            for column, offset, offsets in pieces
        ]

    s_left, s_right = halo_copies(sb, pieces_left, 3, left), halo_copies(sb, pieces_right, 0, right)
    z_left, z_right = halo_copies(zb, pieces_left, 3, left), halo_copies(zb, pieces_right, 0, right)
    z_edge_left = halo_copies(zb, edge_left, 3, left)
    z_edge_right = halo_copies(zb, edge_right, 0, right)

    def mask_own(which, band):
        for column in range(COLS):
            loads[which, column].wait()
        for column in range(COLS):
            half = column % 2
            for offset in range(OFFS):
                if offset == W:
                    continue
                scale = present(column, offset)
                row = column + offset - W
                if which == 1 and row < 0:
                    scale = scale * first
                if which == 1 and row >= COLS:
                    scale = scale * last
                scale_block(band, place(1 + column // 2, half, half + offset), scale)

    pattern_copy.wait()
    mask_own(0, sb)
    pl.semaphore_wait(barrier, len(near_by))

    @pl.when(inner_left)
    def _():
        all_start(s_left)

    @pl.when(inner_right)
    def _():
        all_start(s_right)

    signal(known.at[0], along_y(1), along_y(-1))
    signal(known.at[3], along_z(1), along_z(-1))
    mask_own(1, zb)

    @pl.when(inner_left)
    def _():
        all_start(z_left)

    @pl.when(jnp.logical_not(inner_left))
    def _():
        all_start(z_edge_left)

    @pl.when(inner_right)
    def _():
        all_start(z_right)

    @pl.when(jnp.logical_not(inner_right))
    def _():
        all_start(z_edge_right)

    pl.semaphore_wait(known.at[0], 2)
    signal(known.at[1], mate)
    pl.semaphore_wait(known.at[3], 2)
    signal(known.at[4], along_z(2), along_z(-2))

    def flip(inner, outer):
        value = zb[outer + 1, pl.ds((inner - outer + 1) * SUP, SUP), :]
        zt[inner + 1, pl.ds((outer - inner + 1) * SUP, SUP), :] = value.T

    for outer in (0, 1):
        for inner in (outer - 1, outer, outer + 1):
            flip(inner, outer)

    def upper(column):
        return dot(zt[column, pl.ds(2 * SUP, SUP), :], sb[column + 1, pl.ds(0, SUP), :])

    def lower(column):
        return dot(zt[column + 2, pl.ds(0, SUP), :], sb[column + 1, pl.ds(2 * SUP, SUP), :])

    t_left, t_right = [remote(ts.at[0], td.at[1], left)], [remote(ts.at[1], tu.at[0], right)]
    ts[0] = lower(0).astype(jnp.bfloat16)

    @pl.when(inner_left)
    def _():
        all_start(t_left)

    ts[1] = upper(1).astype(jnp.bfloat16)

    @pl.when(inner_right)
    def _():
        all_start(t_right)

    tu[1] = upper(0).astype(jnp.bfloat16)
    td[0] = lower(1).astype(jnp.bfloat16)

    def near(bands, values, own, row, inners):
        total = None
        for inner in inners:
            if abs(row - inner) > 1:
                continue
            term = dot(
                bands[own + inner, pl.ds((row - inner + 1) * SUP, SUP), :],
                values[pl.ds(inner * SUP, SUP), :],
            )
            total = term if total is None else total + term
        return total

    local = {0: (1, 2), 1: (0, 1)}
    halo = {0: 0, 1: 2}

    for own in (0, 1):
        for row in range(3):
            acc[own, pl.ds(row * SUP, SUP), :] = near(sb, zb.at[own + 1], own, row, local[own])

    pl.semaphore_wait(known.at[1], 1)
    signal(known.at[2], along_x(1), along_x(-1))
    pl.semaphore_wait(known.at[4], 2)
    signal(known.at[5], along_z(4), along_z(-4))

    @pl.when(inner_left)
    def _():
        all_arrived(s_right)

    @pl.when(inner_right)
    def _():
        all_arrived(s_left)

    for own in (0, 1):
        for row in range(3):
            where = (own, pl.ds(row * SUP, SUP), slice(None))
            total = acc[where]
            extra = near(sb, zb.at[own + 1], own, row, (halo[own],))
            if extra is not None:
                total = total + extra
            pb[where] = total.astype(jnp.bfloat16)

    eye = (
        lax.broadcasted_iota(jnp.int32, (B, B), 0) == lax.broadcasted_iota(jnp.int32, (B, B), 1)
    ).astype(jnp.float32)

    def blocks_of(own, row):
        for r in range(2):
            for c in range(2):
                offset = 2 * row + r - c
                if 0 <= offset < OFFS:
                    yield r, c, 2 * own + c, offset

    squares = jnp.zeros((8, B), jnp.float32)

    def defect(own, row, total, squares):
        for r, c, column, offset in blocks_of(own, row):
            block = -total[r * B : (r + 1) * B, c * B : (c + 1) * B]
            if offset == W:
                block = eye + block
            else:
                block = block * present(column, offset)
            block = block.astype(jnp.bfloat16)
            db[own + 1, pl.ds((2 * row + r) * B, B), pl.ds(c * B, B)] = block
            wide = block.astype(jnp.float32)
            squares = squares + jnp.sum((wide * wide).reshape(B // 8, 8, B), axis=0)
        return squares

    def outer(own, row):
        corner = (tu, td)[row // 2]
        return dot(corner[own], zb[own + 1, pl.ds(row * SUP, SUP), :])

    for own, rows in ((0, (1, 2)), (1, (0, 1))):
        for row in rows:
            total = near(zt, pb.at[own], own, row, (0, 1, 2))
            if row != 1:
                total = total + outer(own, row)
            squares = defect(own, row, total, squares)

    pl.semaphore_wait(known.at[2], 2)
    signal(known.at[6], along_x(2))
    pl.semaphore_wait(known.at[5], 2)

    @pl.when(inner_left)
    def _():
        all_arrived(z_right)

    @pl.when(jnp.logical_not(inner_left))
    def _():
        all_arrived(z_edge_right)

    @pl.when(inner_right)
    def _():
        all_arrived(z_left)

    @pl.when(jnp.logical_not(inner_right))
    def _():
        all_arrived(z_edge_left)

    flip(-1, -1)
    flip(0, -1)
    flip(1, 2)
    flip(2, 2)
    edges = ((0, 0), (1, 2))
    for own, row in edges:
        acc[own, pl.ds(row * SUP, SUP), :] = near(zt, pb.at[own], own, row, (0, 1, 2))
    @pl.when(inner_left)
    def _():
        all_arrived(t_right)

    @pl.when(inner_right)
    def _():
        all_arrived(t_left)

    for own, row in edges:
        total = acc[own, pl.ds(row * SUP, SUP), :] + outer(own, row)
        squares = defect(own, row, total, squares)

    part_a[in_plane] = jnp.sum(squares, axis=0, keepdims=True)
    pl.semaphore_wait(known.at[6], 1)

    def sum_copy(buffer, slot, stage, peer):
        return pltpu.make_async_remote_copy(
            src_ref=buffer.at[slot],
            dst_ref=buffer.at[slot],
            send_sem=sum_send.at[stage],
            recv_sem=sum_recv.at[stage],
            device_id=peer,
            device_id_type=MESH,
        )

    def hops(step, size):
        return min(step, size - step)

    plane_steps = sorted(
        ((x, y, c) for x in range(n_grp) for y in range(n_row) for c in range(2) if x or y or c),
        key=lambda step: -hops(step[0], n_grp) - hops(step[1], n_row),
    )
    z_steps = sorted(range(1, n_z), key=lambda step: -hops(step, n_z))

    def all_of(buffer, rows, sem):
        return pltpu.make_async_copy(buffer.at[pl.ds(0, rows)], buffer.at[pl.ds(0, rows)], sem)

    x_of = [lax.rem(grp + step, n_grp) for step in range(n_grp)]
    y_of = [z_here * PLANE + 2 * lax.rem(row_here + step, n_row) for step in range(n_row)]
    core_of = (core, 1 - core)
    for x, y, c in plane_steps:
        sum_copy(part_a, in_plane, 0, (x_of[x], y_of[y] + core_of[c])).start()
    d_halo = [
        remote(
            db.at[index, pl.ds(first_row, rows), pl.ds(half * B, B)],
            db.at[target, pl.ds(first_row, rows), pl.ds(half * B, B)],
            peer,
        )
        for index, target, peer, half, first_row, rows in (
            (1, 3, left, 0, 0, 4 * B),
            (2, 0, right, 1, 2 * B, 4 * B),
            (1, 3, left, 1, B, 3 * B),
            (2, 0, right, 0, 2 * B, 3 * B),
        )
    ]
    all_start(d_halo)

    for own in (0, 1):
        for row in range(3):
            where = (own, pl.ds(row * SUP, SUP), slice(None))
            acc[where] = near(zb, db.at[own + 1], own, row, (0, 1, 2))
            acc2[where] = near(db, db.at[own + 1], own, row, local[own])

    all_of(part_a, n_plane - 1, sum_recv.at[0]).wait()
    part_b[z_here] = jnp.sum(part_a[...], axis=0)
    for step in z_steps:
        sum_copy(part_b, z_here, 1, along_z(step)).start()

    all_arrived(d_halo)
    for own in (0, 1):
        for row in range(3):
            total = acc2[own, pl.ds(row * SUP, SUP), :]
            extra = near(db, db.at[own + 1], own, row, (halo[own],))
            if extra is not None:
                total = total + extra
            for r, c, column, offset in blocks_of(own, row):
                block = total[r * B : (r + 1) * B, c * B : (c + 1) * B]
                block = (block * present(column, offset)).astype(jnp.bfloat16)
                eb[own, pl.ds((2 * row + r) * B, B), pl.ds(c * B, B)] = block

    for own in (0, 1):
        for row in range(3):
            total = 0.375 * near(zb, eb.at[own], own, row, (0, 1, 2))
            total = total + 0.5 * acc[own, pl.ds(row * SUP, SUP), :]
            for r, c, column, offset in blocks_of(own, row):
                block = total[r * B : (r + 1) * B, c * B : (c + 1) * B]
                base = zb[own + 1, pl.ds((2 * row + r) * B, B), pl.ds(c * B, B)]
                block = (block + base.astype(jnp.float32)) * present(column, offset)
                out[column, offset] = block.astype(jnp.bfloat16)

    @pl.when(inner_right)
    def _():
        all_sent(s_right + z_right + t_right)

    @pl.when(jnp.logical_not(inner_right))
    def _():
        all_sent(z_edge_right)

    @pl.when(inner_left)
    def _():
        all_sent(s_left + z_left + t_left)

    @pl.when(jnp.logical_not(inner_left))
    def _():
        all_sent(z_edge_left)

    all_sent(d_halo)
    all_of(part_a, n_plane - 1, sum_send.at[0]).wait()
    all_of(part_b, n_z - 1, sum_send.at[1]).wait()

    all_of(part_b, n_z - 1, sum_recv.at[1]).wait()
    total = jnp.sum(jnp.sum(part_b[...], axis=0), axis=1, keepdims=True)
    norm[...] = jnp.broadcast_to(jnp.sqrt(total / (count * COLS * B)), (8, B))


def finish(refined, norm, refined_out, norm_out, cell, sem):
    cell[...] = norm[0:1, 0:1]
    copies = [pltpu.make_async_copy(cell, norm_out, sem.at[COLS])]
    for column in range(COLS):
        copies.append(
            pltpu.make_async_copy(refined.at[column], refined_out.at[column], sem.at[column])
        )
    for copy in copies:
        copy.start()
    for copy in copies:
        copy.wait()


def in_hbm(array):
    return pltpu.with_memory_space_constraint(array, pltpu.HBM)


def solution(mesh):
    n_grp, n_slab = mesh.shape["grp"], mesh.shape["slab"]
    n_plane, n_z = n_grp * PLANE, n_slab // PLANE

    def step(margin, factor, pattern):
        bands = pltpu.VMEM((4, BAND, SUP), jnp.bfloat16)
        pairs = pltpu.VMEM((2, BAND, SUP), jnp.bfloat16)
        wide = pltpu.VMEM((2, BAND, SUP), jnp.float32)
        corner = pltpu.VMEM((2, SUP, SUP), jnp.bfloat16)
        refined, norm = pl.pallas_call(
            functools.partial(kernel, n_grp, n_slab),
            out_shape=(
                jax.ShapeDtypeStruct((COLS, OFFS, B, B), jnp.bfloat16),
                jax.ShapeDtypeStruct((8, B), jnp.float32),
            ),
            in_specs=[
                pl.BlockSpec(memory_space=pltpu.HBM),
                pl.BlockSpec(memory_space=pltpu.HBM),
                pl.BlockSpec(memory_space=pltpu.HBM),
            ],
            out_specs=(
                pl.BlockSpec(memory_space=pltpu.VMEM),
                pl.BlockSpec(memory_space=pltpu.VMEM),
            ),
            scratch_shapes=[
                bands,
                bands,
                bands,
                pairs,
                bands,
                pairs,
                corner,
                corner,
                corner,
                wide,
                wide,
                pltpu.VMEM((n_plane, 1, B), jnp.float32),
                pltpu.VMEM((n_z, 1, B), jnp.float32),
                pltpu.SemaphoreType.DMA((2 * COLS,)),
                pltpu.SemaphoreType.DMA((COPIES,)),
                pltpu.SemaphoreType.DMA((COPIES,)),
                pltpu.SemaphoreType.DMA((2,)),
                pltpu.SemaphoreType.DMA((2,)),
                pltpu.SemaphoreType.REGULAR((7,)),
                pltpu.SMEM((COLS, OFFS), jnp.int32),
                pltpu.SemaphoreType.DMA,
            ],
            compiler_params=pltpu.CompilerParams(
                collective_id=0, has_side_effects=True, vmem_limit_bytes=24 << 20
            ),
        )(
            in_hbm(margin.reshape(COLS, OFFS * B, B)),
            in_hbm(factor.reshape(COLS, OFFS * B, B)),
            in_hbm(pattern),
        )
        refined, norm = pl.pallas_call(
            finish,
            out_shape=(
                jax.ShapeDtypeStruct((COLS, OFFS, B, B), jnp.bfloat16),
                jax.ShapeDtypeStruct((1, 1), jnp.float32),
            ),
            in_specs=[pl.BlockSpec(memory_space=pltpu.VMEM)] * 2,
            out_specs=(pl.BlockSpec(memory_space=pl.ANY), pl.BlockSpec(memory_space=pl.ANY)),
            scratch_shapes=[
                pltpu.VMEM((1, 1), jnp.float32),
                pltpu.SemaphoreType.DMA((COLS + 1,)),
            ],
            compiler_params=pltpu.CompilerParams(vmem_limit_bytes=8 << 20),
        )(refined, norm)
        return refined, norm.reshape(())

    return jax.shard_map(
        step,
        mesh=mesh,
        in_specs=(
            P(("grp", "slab"), None, None, None),
            P(("grp", "slab"), None, None, None),
            P(("grp", "slab"), None),
        ),
        out_specs=(P(("grp", "slab"), None, None, None), P()),
        check_vma=False,
    )
```
